32 devices in a mesh: dom: 8 (over z, y), rows: 4 (over x, core).
Axes of the slice: x: 2, y: 2, z: 4, core: 2. Of those that a mesh axis runs over, the one named last changes fastest.
Arguments:
- fields: float32 [8, 3, 128, 4096], P('dom', None, 'rows'), may hold values from -6 to 6
- depth: float32 [128, 4096], P('rows'), may hold values from 1.5 to 6
- obs_index: int32 [256], replicated, may hold values from 0 to 524287, as said below
- obs_value: float32 [256], replicated, may hold values from -6 to 6
- obs_var: float32 [256], replicated, may hold values from 0.5 to 5
- parent_lookup: int32 [8], replicated, may hold values from 0 to 7, as said below
Outputs:
- log_weights: float32 [8], P('dom')
- posterior_members: float32 [8, 3, 128, 4096], P('dom', None, 'rows')
The draws below stay inside these ranges and needn't reach their ends.
Inputs may be any that keep to these rules, and one draw needn't show every extreme that they name: `parent_lookup`: every value is the index of a particle; 0 and 7 each appear; values may repeat. `obs_index`: indices of grid cells, possibly repeated; the first and last cell each appear.
All inputs are finite; a program needn't handle non-finite values.
Results may differ from the reference program's by a relative error of at most 0.00003.
Values sent between devices are 32-bit elements; how exact they have to be, the bound alone decides.
No kernel may reach another device: no remote copies, remote signals or barrier semaphores. Data moves between devices by JAX's collectives and lax.ppermute only.
A program may use at most 64 MiB of HBM per device.

```python
import math
import jax
import jax.numpy as jnp

NCOL = 4096
STEPS = 4
NOBS = 256
PARTICLES = 8
NROWS = 128


def draw_parent_lookup(key, part):
    first, second = jax.random.split(jax.random.fold_in(key, 11))
    values = jax.random.randint(first, (PARTICLES,), 0, PARTICLES)
    order = jax.random.permutation(second, PARTICLES)
    values = values.at[order[0]].set(0)
    values = values.at[order[1]].set(PARTICLES - 1)
    return values.astype(jnp.int32)


def draw_obs_index(key, part):
    first, second = jax.random.split(jax.random.fold_in(key, 23))
    values = jax.random.randint(first, (NOBS,), 0, NROWS * NCOL)
    order = jax.random.permutation(second, NOBS)
    values = values.at[order[0]].set(0)
    values = values.at[order[1]].set(NROWS * NCOL - 1)
    return values.astype(jnp.int32)


def shard_levels(key, dims, cuts, smallest, top_value):
    factor_of, own = 1.0, jax.random.fold_in(key, 6)
    for position, shards_of in cuts:
        draws = jnp.exp(jax.random.uniform(jax.random.fold_in(own, position), (shards_of,), jnp.float32, smallest / len(cuts), top_value / len(cuts)))
        factor_of = factor_of * jnp.repeat(draws, dims[position] // shards_of).reshape([-1 if axis == position else 1 for axis in range(len(dims))])
    return factor_of


def normal_values(own_key, dims, spread, most, cuts=(), dtype=jnp.bfloat16):
    level = shard_levels(own_key, dims, cuts, -0.22, 0.18) if cuts else 1.0
    entries = jax.random.normal(own_key, dims, jnp.float32) * spread * level
    return jnp.minimum(jnp.maximum(entries, -most), most).astype(dtype)


def setup_inputs(seed: int = 0) -> dict:
    key_of = jax.random.split(jax.random.key(seed), 7)
    fields = normal_values(key_of[0], (PARTICLES, 3, NROWS, NCOL), 1.0, 6.0, ((0, 8), (2, 4)), jnp.float32)
    depth = jnp.clip(jnp.exp(math.log(6.0) - 1.3862944 * jax.random.uniform(key_of[1], (NROWS, NCOL), jnp.float32) ** shard_levels(key_of[1], (NROWS, NCOL), ((0, 4),), -0.2, 0.2)), 1.5, 6.0)
    obs_index = draw_obs_index(jax.random.fold_in(key_of[6], 71), 0)
    obs_value = normal_values(key_of[3], (NOBS,), 1.0, 6.0, (), jnp.float32)
    obs_var = jnp.clip(jnp.exp(jax.random.uniform(key_of[4], (NOBS,), jnp.float32, math.log(0.5), math.log(5.0))), 0.5, 5.0)
    parent_lookup = draw_parent_lookup(jax.random.fold_in(key_of[6], 71), 0)
    return dict(fields=fields, depth=depth, obs_index=obs_index, obs_value=obs_value, obs_var=obs_var, parent_lookup=parent_lookup)


time_step = 0.5
coriolis = 0.2


def rows_diff(a):
    padded = jnp.pad(a, ((0, 0), (1, 1), (0, 0)))
    return 0.5 * (padded[:, 2:] - padded[:, :-2])


def cols_diff(a):
    return 0.5 * (jnp.roll(a, -1, axis=-1) - jnp.roll(a, 1, axis=-1))


def reference(fields, depth, obs_index, obs_value, obs_var, parent_lookup):
    free_elevation = fields[:, 0]
    zonal_current = fields[:, 1]
    meridional_current = fields[:, 2]
    for step in range(STEPS):
        free_elevation = free_elevation - time_step * (cols_diff(depth * zonal_current) + rows_diff(depth * meridional_current))
        zonal_current = zonal_current - time_step * cols_diff(free_elevation) + time_step * coriolis * meridional_current
        meridional_current = meridional_current - time_step * rows_diff(free_elevation) - time_step * coriolis * zonal_current
    prior_members = jnp.stack([free_elevation, zonal_current, meridional_current], axis=1)
    flat = free_elevation.reshape(free_elevation.shape[0], -1)
    values = jnp.take(flat, obs_index, axis=1)
    loglik = -0.5 * jnp.sum((obs_value[None, :] - values) ** 2 / obs_var[None, :], axis=1)
    peak = jnp.max(loglik)
    total = jnp.sum(jnp.exp(loglik - peak))
    log_weights = loglik - (peak + jnp.log(total))
    posterior_members = jnp.take(prior_members, parent_lookup, axis=0)
    return log_weights, posterior_members
```

```python
import jax
import jax.numpy as jnp
from jax import lax
from jax.experimental import pallas as pl
from jax.experimental.pallas import tpu as pltpu
from jax.sharding import PartitionSpec as P

STEPS = 4
HALO = 2 * STEPS
LANES = 128

time_step = 0.5
coriolis = 0.2


def forecast_steps(h, u, v, d, top_open, bottom_open):
    n_rows, n_cols = h.shape
    for _ in range(STEPS):
        du = d * u
        dv = d * v
        dx = 0.5 * (pltpu.roll(du, n_cols - 1, 1) - pltpu.roll(du, 1, 1))
        dy = 0.5 * (pltpu.roll(dv, n_rows - 1, 0) - pltpu.roll(dv, 1, 0))
        h = h - time_step * (dx + dy)
        h = jnp.concatenate(
            [h[:HALO] * top_open, h[HALO : n_rows - HALO], h[n_rows - HALO :] * bottom_open], axis=0
        )
        dx = 0.5 * (pltpu.roll(h, n_cols - 1, 1) - pltpu.roll(h, 1, 1))
        u = u - time_step * dx + (time_step * coriolis) * v
        dy = 0.5 * (pltpu.roll(h, n_rows - 1, 0) - pltpu.roll(h, 1, 0))
        v = v - time_step * dy - (time_step * coriolis) * u
    return h, u, v


def forecast_kernel(open_ref, fields_ref, depth_ref, above_ref, below_ref, out_ref, *, width, piece):
    n_cols = fields_ref.shape[-1]
    n_rows = fields_ref.shape[-2]
    top_open = open_ref[0].astype(jnp.float32)
    bottom_open = open_ref[1].astype(jnp.float32)
    lane = lax.broadcasted_iota(jnp.int32, (n_rows + 2 * HALO, LANES), 1)

    def chunk(c, carry):
        start = pl.multiple_of(c * width, LANES)
        left = pl.multiple_of(jnp.where(c == 0, n_cols, start) - LANES, LANES)
        right = pl.multiple_of(jnp.where(start + width == n_cols, 0, start + width), LANES)

        def rows_of(k, at, size):
            mid = depth_ref[:, pl.ds(at, size)] if k == 3 else fields_ref[0, k, :, pl.ds(at, size)]
            return jnp.concatenate(
                [above_ref[k, :, pl.ds(at, size)], mid, below_ref[k, :, pl.ds(at, size)]], axis=0
            )

        def window(k):
            rim = jnp.where(lane < LANES // 2, rows_of(k, right, LANES), rows_of(k, left, LANES))
            return jnp.concatenate([rows_of(k, start, width), rim], axis=1)

        done = forecast_steps(window(0), window(1), window(2), window(3), top_open, bottom_open)
        for k in range(3):
            for q in range(width // piece):
                out_ref[c * (width // piece) + q, k] = done[k][HALO : HALO + n_rows, q * piece : (q + 1) * piece]
        return carry

    lax.fori_loop(0, n_cols // width, chunk, 0)


def forecast(fields, depth, above, below, opens, pieces):
    n_rows, n_cols = depth.shape
    piece = n_cols // pieces
    width = max(512, piece)
    vmem = pl.BlockSpec(memory_space=pltpu.VMEM)
    return pl.pallas_call(
        lambda *refs: forecast_kernel(*refs, width=width, piece=piece),
        out_shape=jax.ShapeDtypeStruct((pieces, 3, n_rows, piece), jnp.float32),
        in_specs=[pl.BlockSpec(memory_space=pltpu.SMEM), vmem, vmem, vmem, vmem],
        out_specs=vmem,
        compiler_params=pltpu.CompilerParams(vmem_limit_bytes=48 * 2**20),
        name="forecast",
    )(opens, fields, depth, above, below)


def copy_block(parents_ref, src_ref, dst_ref):
    dst_ref[...] = src_ref[...]


def pick(received, parent_lookup):
    slots = parent_lookup.shape[0]
    block = (1,) + received.shape[1:]
    return pl.pallas_call(
        copy_block,
        grid_spec=pltpu.PrefetchScalarGridSpec(
            num_scalar_prefetch=1,
            grid=(slots,),
            in_specs=[pl.BlockSpec(block, lambda i, parents: (parents[i], 0, 0, 0))],
            out_specs=pl.BlockSpec(block, lambda i, parents: (i, 0, 0, 0)),
        ),
        out_shape=jax.ShapeDtypeStruct((slots,) + received.shape[1:], received.dtype),
        name="pick",
    )(parent_lookup, received)


def place_block(src_ref, dst_ref):
    dst_ref[...] = src_ref[...]


def place(pieces):
    count, comps, n_rows, piece = pieces.shape
    block = (1, comps, n_rows, piece)
    return pl.pallas_call(
        place_block,
        grid=(count,),
        in_specs=[pl.BlockSpec(block, lambda j: (j, 0, 0, 0))],
        out_specs=pl.BlockSpec(block, lambda j: (0, 0, 0, j)),
        out_shape=jax.ShapeDtypeStruct((1, comps, n_rows, count * piece), pieces.dtype),
        name="place",
    )(pieces)


def sum_over(x, axis):
    count = lax.axis_size(axis)
    step = 1
    while step < count:
        x = x + lax.ppermute(x, axis, [(i, i ^ step) for i in range(count)])
        step *= 2
    return x


def log_weight(pieces, obs_index, obs_value, obs_var):
    count, _, n_rows, piece = pieces.shape
    n_cols = count * piece
    slab = n_rows * n_cols
    offset = obs_index - lax.axis_index("rows") * slab
    inside = (offset >= 0) & (offset < slab)
    offset = jnp.clip(offset, 0, slab - 1)
    row = offset // n_cols
    col = offset % n_cols
    values = pieces[:, 0].at[col // piece, row, col % piece].get(mode="promise_in_bounds")
    misfit = jnp.sum(jnp.where(inside, (obs_value - values) ** 2 / obs_var, 0.0))
    loglik = sum_over(-0.5 * misfit, "rows")
    slots = lax.broadcasted_iota(jnp.int32, (lax.axis_size("dom"),), 0)
    every = sum_over(jnp.where(slots == lax.axis_index("dom"), loglik, 0.0), "dom")
    peak = jnp.max(every)
    total = jnp.sum(jnp.exp(every - peak))
    return (loglik - (peak + jnp.log(total)))[None]


def shards(fields, depth, obs_index, obs_value, obs_var, parent_lookup):
    count = lax.axis_size("rows")
    pieces = lax.axis_size("dom")
    head = jnp.concatenate([fields[0, :, :HALO], depth[None, :HALO]], axis=0)
    tail = jnp.concatenate([fields[0, :, -HALO:], depth[None, -HALO:]], axis=0)
    above = lax.ppermute(tail, "rows", [(i, i + 1) for i in range(count - 1)])
    below = lax.ppermute(head, "rows", [(i + 1, i) for i in range(count - 1)])
    at = lax.axis_index("rows")
    opens = jnp.stack([at > 0, at < count - 1]).astype(jnp.int32)
    prior = forecast(fields, depth, above, below, opens, pieces)
    received = lax.all_to_all(prior, "dom", split_axis=0, concat_axis=0, tiled=True)
    log_weights = log_weight(prior, obs_index, obs_value, obs_var)
    picked = pick(received, parent_lookup)
    final = lax.all_to_all(picked, "dom", split_axis=0, concat_axis=0, tiled=True)
    return log_weights, place(final)


def solution(mesh):
    in_specs = (P("dom", None, "rows", None), P("rows", None), P(), P(), P(), P())
    out_specs = (P("dom"), P("dom", None, "rows", None))
    return jax.shard_map(shards, mesh=mesh, in_specs=in_specs, out_specs=out_specs, check_vma=False)
```

```python
import jax
import jax.numpy as jnp
from jax import lax
from jax.experimental import pallas as pl
from jax.experimental.pallas import tpu as pltpu
from jax.sharding import PartitionSpec as P

STEPS = 4
HALO = 2 * STEPS
LANES = 128
VMEM_BYTES = 48 * 2**20

time_step = 0.5
coriolis = 0.2

in_vmem = pl.BlockSpec(memory_space=pltpu.VMEM)
in_smem = pl.BlockSpec(memory_space=pltpu.SMEM)
in_any = pl.BlockSpec(memory_space=pl.ANY)


def forecast_steps(h, u, v, d, top_open=None, bottom_open=None):
    n_rows, n_cols = h.shape
    for _ in range(STEPS):
        du = d * u
        dv = d * v
        dx = 0.5 * (pltpu.roll(du, n_cols - 1, 1) - pltpu.roll(du, 1, 1))
        dy = 0.5 * (pltpu.roll(dv, n_rows - 1, 0) - pltpu.roll(dv, 1, 0))
        h = h - time_step * (dx + dy)
        if top_open is not None:
            h = jnp.concatenate(
                [h[:HALO] * top_open, h[HALO : n_rows - HALO], h[n_rows - HALO :] * bottom_open], axis=0
            )
        dx = 0.5 * (pltpu.roll(h, n_cols - 1, 1) - pltpu.roll(h, 1, 1))
        u = u - time_step * dx + (time_step * coriolis) * v
        dy = 0.5 * (pltpu.roll(h, n_rows - 1, 0) - pltpu.roll(h, 1, 0))
        v = v - time_step * dy - (time_step * coriolis) * u
    return h, u, v


def chunk_width(n_cols, piece):
    return min(512, piece)


def window_columns(rows_of, start, width, n_cols, n_rows):
    left = pl.multiple_of(lax.rem(start + n_cols - LANES, n_cols), LANES)
    right = pl.multiple_of(lax.rem(start + width, n_cols), LANES)
    lane = lax.broadcasted_iota(jnp.int32, (n_rows, LANES), 1)

    def window(k):
        rim = jnp.where(lane < LANES // 2, rows_of(k, right, LANES), rows_of(k, left, LANES))
        return jnp.concatenate([rows_of(k, start, width), rim], axis=1)

    return [window(k) for k in range(4)]


def over_pieces(at_ref, n_cols, outs, work):
    piece = n_cols // len(outs)
    width = chunk_width(n_cols, piece)
    parts = piece // width

    def part(i, carry):
        m = i // parts
        inner = pl.multiple_of(i % parts * width, LANES)
        start = pl.multiple_of(jnp.bitwise_xor(at_ref[0], m) * piece + inner, LANES)
        done = work(start, width)
        for to, out in enumerate(outs):

            @pl.when(m == to)
            def _(out=out):
                for k in range(3):
                    out[k, :, pl.ds(inner, width)] = done[k]

        return carry

    lax.fori_loop(0, len(outs) * parts, part, 0)


def inner_kernel(at_ref, fields_ref, depth_ref, *refs):
    outs, h_ref = refs[:-1], refs[-1]
    n_rows, n_cols = depth_ref.shape

    def rows_of(k, at, size):
        return depth_ref[:, pl.ds(at, size)] if k == 3 else fields_ref[0, k, :, pl.ds(at, size)]

    def work(start, width):
        done = forecast_steps(*window_columns(rows_of, start, width, n_cols, n_rows))
        done = [x[HALO : n_rows - HALO, :width] for x in done]
        h_ref[:, pl.ds(start, width)] = done[0]
        return done

    over_pieces(at_ref, n_cols, outs, work)


def outer_kernel(at_ref, fields_ref, depth_ref, above_ref, below_ref, *refs):
    outs, h_ref = refs[:-1], refs[-1]
    n_rows, n_cols = depth_ref.shape
    top_open = at_ref[1].astype(jnp.float32)
    bottom_open = at_ref[2].astype(jnp.float32)

    def rows_of(k, at, size):
        mid = depth_ref[:, pl.ds(at, size)] if k == 3 else fields_ref[0, k, :, pl.ds(at, size)]
        return jnp.concatenate([above_ref[k, :, pl.ds(at, size)], mid, below_ref[k, :, pl.ds(at, size)]], axis=0)

    def work(start, width):
        columns = window_columns(rows_of, start, width, n_cols, n_rows + 2 * HALO)
        done = forecast_steps(*columns, top_open, bottom_open)
        done = [jnp.concatenate([x[HALO : 2 * HALO, :width], x[n_rows : n_rows + HALO, :width]], axis=0) for x in done]
        h_ref[:, pl.ds(start, width)] = done[0]
        return done

    over_pieces(at_ref, n_cols, outs, work)


def forecast(kernel, name, at, arrays, n_rows, n_cols, count):
    piece = jax.ShapeDtypeStruct((3, n_rows, n_cols // count), jnp.float32)
    outs = pl.pallas_call(
        kernel,
        out_shape=[piece] * count + [jax.ShapeDtypeStruct((n_rows, n_cols), jnp.float32)],
        in_specs=[in_smem] + [in_vmem] * len(arrays),
        out_specs=[in_vmem] * (count + 1),
        compiler_params=pltpu.CompilerParams(vmem_limit_bytes=VMEM_BYTES),
        name=name,
    )(at, *arrays)
    return outs[:-1], outs[-1]


def misfit_kernel(at_ref, index_ref, value_ref, var_ref, inner_ref, outer_ref, out_ref):
    inner_rows, n_cols = inner_ref.shape
    n_rows = inner_rows + 2 * HALO
    base = at_ref[3] * (n_rows * n_cols)
    row_in = lax.broadcasted_iota(jnp.int32, (8, LANES), 0)
    lane_in = lax.broadcasted_iota(jnp.int32, (8, LANES), 1)

    def tile(ref, row, col):
        return ref[pl.ds(pl.multiple_of(row // 8 * 8, 8), 8), pl.ds(pl.multiple_of(col // LANES * LANES, LANES), LANES)]

    def point(k, total):
        offset = index_ref[k] - base
        inside = jnp.logical_and(offset >= 0, offset < n_rows * n_cols)
        offset = jnp.where(inside, offset, 0)
        row = offset // n_cols
        col = offset - row * n_cols
        is_inner = jnp.logical_and(row >= HALO, row < n_rows - HALO)
        inner_row = jnp.clip(row - HALO, 0, inner_rows - 1)
        outer_row = jnp.clip(jnp.where(row < HALO, row, row - inner_rows), 0, 2 * HALO - 1)
        seen = jnp.where(is_inner, tile(inner_ref, inner_row, col), tile(outer_ref, outer_row, col))
        hit = (row_in == row % 8) & (lane_in == jnp.where(inside, col % LANES, -1))
        return total + jnp.where(hit, (value_ref[k] - seen) ** 2 / var_ref[k], 0.0)

    total = lax.fori_loop(0, index_ref.shape[0], point, jnp.zeros((8, LANES), jnp.float32), unroll=8)
    out_ref[...] = jnp.broadcast_to(jnp.sum(total), out_ref.shape)


def misfit(at, obs_index, obs_value, obs_var, inner, outer):
    return pl.pallas_call(
        misfit_kernel,
        out_shape=jax.ShapeDtypeStruct((8, LANES), jnp.float32),
        in_specs=[in_smem] * 4 + [in_vmem] * 2,
        out_specs=in_vmem,
        compiler_params=pltpu.CompilerParams(vmem_limit_bytes=VMEM_BYTES),
        name="misfit",
    )(at, obs_index, obs_value, obs_var, inner, outer)[0, 0]


def sum_over(x, axis):
    count = lax.axis_size(axis)
    step = 1
    while step < count:
        x = x + lax.ppermute(x, axis, [(i, i ^ step) for i in range(count)])
        step *= 2
    return x


def log_weight(misfit_sum):
    loglik = sum_over(-0.5 * misfit_sum, "rows")
    slots = lax.broadcasted_iota(jnp.int32, (lax.axis_size("dom"),), 0)
    every = sum_over(jnp.where(slots == lax.axis_index("dom"), loglik, 0.0), "dom")
    peak = jnp.max(every)
    total = jnp.sum(jnp.exp(every - peak))
    return (loglik - (peak + jnp.log(total)))[None]


def place(at, pieces, spans, shape, into=None):
    count = len(pieces)
    n_cols = shape[-1]
    width = n_cols // count

    def kernel(at_ref, *refs):
        srcs = refs[:count]
        dst, sems = refs[-2], refs[-1]
        copies = []
        for m in range(count):
            first = pl.multiple_of(jnp.bitwise_xor(at_ref[0], m) * width, LANES)
            for s, (src_row, dst_row, size) in enumerate(spans):
                copies.append(
                    pltpu.make_async_copy(
                        srcs[m].at[:, pl.ds(src_row, size), :],
                        dst.at[0, :, pl.ds(dst_row, size), pl.ds(first, width)],
                        sems.at[m * len(spans) + s],
                    )
                )
        for c in copies:
            c.start()
        for c in copies:
            c.wait()

    extra = [] if into is None else [into]
    return pl.pallas_call(
        kernel,
        out_shape=jax.ShapeDtypeStruct(shape, jnp.float32),
        in_specs=[in_smem] + [in_any] * (count + len(extra)),
        out_specs=in_any,
        scratch_shapes=[pltpu.SemaphoreType.DMA((count * len(spans),))],
        input_output_aliases={} if into is None else {count + 1: 0},
        name="place",
    )(at, *pieces, *extra)


def route_kernel(at_ref, parents_ref, out_ref, *, half):
    own = at_ref[0]
    side = at_ref[4]
    parents = [parents_ref[s] for s in range(2 * half)]

    def ranks(first):
        other = half - first
        running = jnp.int32(0)
        needed, rank = [], []
        for q in range(half):
            hit = jnp.int32(0)
            for s in range(half):
                hit = hit | jnp.where(parents[other + s] == first + q, 1, 0).astype(jnp.int32)
            needed.append(hit)
            rank.append(running)
            running = running + hit
        return needed, rank, running

    low = ranks(0)
    high = ranks(half)
    out_ref[0] = jnp.maximum(low[2], high[2])
    mine = [jnp.where(side == 0, a, b) for a, b in zip(low[0], high[0])]
    my_rank = [jnp.where(side == 0, a, b) for a, b in zip(low[1], high[1])]
    other_rank = [jnp.where(side == 0, b, a) for a, b in zip(low[1], high[1])]
    for k in range(half):
        chosen = jnp.int32(0)
        for q in range(half):
            chosen = jnp.where((mine[q] == 1) & (my_rank[q] == k), q, chosen)
        out_ref[1 + k] = jnp.bitwise_xor(chosen, own)
    for m in range(half):
        slot = jnp.bitwise_xor(own, m)
        parent = jnp.int32(0)
        for s in range(half):
            parent = jnp.where(slot == s, jnp.where(side == 0, parents[s], parents[half + s]), parent)
        local = parent - side * half
        remote = parent - (1 - side) * half
        from_rank = jnp.int32(0)
        for q in range(half):
            from_rank = jnp.where(remote == q, other_rank[q], from_rank)
        is_local = jnp.logical_and(local >= 0, local < half)
        out_ref[1 + half + m] = jnp.where(is_local, jnp.bitwise_xor(local, own), half + from_rank)


def route(at, parent_lookup, half):
    return pl.pallas_call(
        lambda *refs: route_kernel(*refs, half=half),
        out_shape=jax.ShapeDtypeStruct((1 + 2 * half,), jnp.int32),
        in_specs=[in_smem, in_smem],
        out_specs=in_smem,
        name="route",
    )(at, parent_lookup)


def to_mate(x, m):
    return lax.ppermute(x, "dom", [(i, i ^ m) for i in range(lax.axis_size("dom"))])


def among_mates(pieces):
    return [x if m == 0 else to_mate(x, m) for m, x in enumerate(pieces)]


def across(held, routes, crossing):
    half = len(held)
    chosen = jnp.stack([lax.select_n(routes[1 + k], *held) for k in range(crossing)])
    got = to_mate(chosen, half)
    return [got[k] for k in range(crossing)]


def for_slots(held, got, routes):
    half = len(held)
    return [lax.select_n(routes[1 + half + m], *held, *got) for m in range(half)]


def halo_rows(fields, depth):
    count = lax.axis_size("rows")
    head = jnp.concatenate([fields[0, :, :HALO], depth[None, :HALO]], axis=0)
    tail = jnp.concatenate([fields[0, :, -HALO:], depth[None, -HALO:]], axis=0)
    above = lax.ppermute(tail, "rows", [(i, i + 1) for i in range(count - 1)])
    below = lax.ppermute(head, "rows", [(i + 1, i) for i in range(count - 1)])
    return above, below


def cycle(crossing, routes, at, fields, depth, obs_index, obs_value, obs_var):
    half = lax.axis_size("dom") // 2
    n_rows, n_cols = depth.shape
    above, below = halo_rows(fields, depth)
    inner, inner_h = forecast(inner_kernel, "inner", at, (fields, depth), n_rows - 2 * HALO, n_cols, half)
    inner_held = among_mates(inner)
    outer, outer_h = forecast(outer_kernel, "outer", at, (fields, depth, above, below), 2 * HALO, n_cols, half)
    outer_held = among_mates(outer)
    log_weights = log_weight(misfit(at, obs_index, obs_value, obs_var, inner_h, outer_h))
    inner_done = among_mates(for_slots(inner_held, across(inner_held, routes, crossing), routes))
    outer_done = among_mates(for_slots(outer_held, across(outer_held, routes, crossing), routes))
    members = place(at, inner_done, ((0, HALO, n_rows - 2 * HALO),), fields.shape)
    members = place(at, outer_done, ((0, 0, HALO), (HALO, n_rows - HALO, HALO)), fields.shape, members)
    return log_weights, members


def shards(fields, depth, obs_index, obs_value, obs_var, parent_lookup):
    rows_at = lax.axis_index("rows")
    dom_at = lax.axis_index("dom")
    half = lax.axis_size("dom") // 2
    at = jnp.stack(
        [dom_at % half, rows_at > 0, rows_at < lax.axis_size("rows") - 1, rows_at, dom_at // half]
    ).astype(jnp.int32)
    if half == 4:
        routes = route(at, parent_lookup, half)
        branches = [
            (lambda r, a, *rest, c=c: cycle(c, r, a, *rest)) for c in range(1, half + 1)
        ]
        return lax.switch(
            jnp.clip(routes[0] - 1, 0, half - 1), branches, routes, at, fields, depth, obs_index, obs_value, obs_var
        )
    return by_pieces(at, fields, depth, obs_index, obs_value, obs_var, parent_lookup)


def by_pieces(at, fields, depth, obs_index, obs_value, obs_var, parent_lookup):
    pieces = lax.axis_size("dom")
    n_rows, n_cols = depth.shape
    above, below = halo_rows(fields, depth)
    whole = at * jnp.array([0, 1, 1, 1, 1], jnp.int32)
    (inner,), inner_h = forecast(inner_kernel, "inner", whole, (fields, depth), n_rows - 2 * HALO, n_cols, 1)
    (outer,), outer_h = forecast(outer_kernel, "outer", whole, (fields, depth, above, below), 2 * HALO, n_cols, 1)
    log_weights = log_weight(misfit(at, obs_index, obs_value, obs_var, inner_h, outer_h))
    slab = jnp.concatenate([outer[:, :HALO], inner, outer[:, HALO:]], axis=1)
    tiles = slab.reshape(3, n_rows, pieces, n_cols // pieces).transpose(2, 0, 1, 3)
    received = lax.all_to_all(tiles, "dom", split_axis=0, concat_axis=0, tiled=True)
    picked = jnp.take(received, parent_lookup, axis=0, mode="clip")
    final = lax.all_to_all(picked, "dom", split_axis=0, concat_axis=0, tiled=True)
    return log_weights, final.transpose(1, 2, 0, 3).reshape(1, 3, n_rows, n_cols)


def solution(mesh):
    in_specs = (P("dom", None, "rows", None), P("rows", None), P(), P(), P(), P())
    out_specs = (P("dom"), P("dom", None, "rows", None))
    return jax.shard_map(shards, mesh=mesh, in_specs=in_specs, out_specs=out_specs, check_vma=False)
```

```python
import jax
import jax.numpy as jnp
from jax import lax
from jax.experimental import pallas as pl
from jax.experimental.pallas import tpu as pltpu
from jax.sharding import PartitionSpec as P

STEPS = 4
HALO = 2 * STEPS
LANES = 128
VMEM_BYTES = 48 * 2**20

time_step = 0.5
coriolis = 0.2

in_vmem = pl.BlockSpec(memory_space=pltpu.VMEM)
in_smem = pl.BlockSpec(memory_space=pltpu.SMEM)
in_hbm = pl.BlockSpec(memory_space=pltpu.HBM)


def forecast_steps(h, u, v, d, top_open=None, bottom_open=None):
    n_rows, n_cols = h.shape
    for _ in range(STEPS):
        du = d * u
        dv = d * v
        dx = 0.5 * (pltpu.roll(du, n_cols - 1, 1) - pltpu.roll(du, 1, 1))
        dy = 0.5 * (pltpu.roll(dv, n_rows - 1, 0) - pltpu.roll(dv, 1, 0))
        h = h - time_step * (dx + dy)
        if top_open is not None:
            h = jnp.concatenate(
                [h[:HALO] * top_open, h[HALO : n_rows - HALO], h[n_rows - HALO :] * bottom_open], axis=0
            )
        dx = 0.5 * (pltpu.roll(h, n_cols - 1, 1) - pltpu.roll(h, 1, 1))
        u = u - time_step * dx + (time_step * coriolis) * v
        dy = 0.5 * (pltpu.roll(h, n_rows - 1, 0) - pltpu.roll(h, 1, 0))
        v = v - time_step * dy - (time_step * coriolis) * u
    return h, u, v


def chunk_width(n_cols, piece):
    return min(512, piece)


def window_columns(rows_of, start, width, n_cols, n_rows):
    left = pl.multiple_of(lax.rem(start + n_cols - LANES, n_cols), LANES)
    right = pl.multiple_of(lax.rem(start + width, n_cols), LANES)
    lane = lax.broadcasted_iota(jnp.int32, (n_rows, LANES), 1)

    def window(k):
        rim = jnp.where(lane < LANES // 2, rows_of(k, right, LANES), rows_of(k, left, LANES))
        return jnp.concatenate([rows_of(k, start, width), rim], axis=1)

    return [window(k) for k in range(4)]


def over_pieces(at_ref, n_cols, outs, work):
    piece = n_cols // len(outs)
    width = chunk_width(n_cols, piece)
    parts = piece // width

    def part(i, carry):
        m = i // parts
        inner = pl.multiple_of(i % parts * width, LANES)
        start = pl.multiple_of(jnp.bitwise_xor(at_ref[0], m) * piece + inner, LANES)
        done = work(start, width)
        for to, out in enumerate(outs):

            @pl.when(m == to)
            def _(out=out):
                for k in range(3):
                    out[k, :, pl.ds(inner, width)] = done[k]

        return carry

    lax.fori_loop(0, len(outs) * parts, part, 0)


def inner_kernel(at_ref, fields_ref, depth_ref, *refs):
    outs, (h_ref, head_ref, tail_ref) = refs[:-3], refs[-3:]
    n_rows, n_cols = depth_ref.shape

    def rows_of(k, at, size):
        return depth_ref[:, pl.ds(at, size)] if k == 3 else fields_ref[0, k, :, pl.ds(at, size)]

    def work(start, width):
        columns = window_columns(rows_of, start, width, n_cols, n_rows)
        for k in range(4):
            head_ref[k, :, pl.ds(start, width)] = columns[k][:HALO, :width]
            tail_ref[k, :, pl.ds(start, width)] = columns[k][n_rows - HALO :, :width]
        done = forecast_steps(*columns)
        done = [x[HALO : n_rows - HALO, :width] for x in done]
        h_ref[:, pl.ds(start, width)] = done[0]
        return done

    over_pieces(at_ref, n_cols, outs, work)


def outer_kernel(at_ref, fields_ref, depth_ref, above_ref, below_ref, *refs):
    outs, h_ref = refs[:-1], refs[-1]
    n_rows, n_cols = depth_ref.shape
    top_open = at_ref[1].astype(jnp.float32)
    bottom_open = at_ref[2].astype(jnp.float32)

    def rows_of(k, at, size):
        mid = depth_ref[:, pl.ds(at, size)] if k == 3 else fields_ref[0, k, :, pl.ds(at, size)]
        return jnp.concatenate([above_ref[k, :, pl.ds(at, size)], mid, below_ref[k, :, pl.ds(at, size)]], axis=0)

    def work(start, width):
        columns = window_columns(rows_of, start, width, n_cols, n_rows + 2 * HALO)
        done = forecast_steps(*columns, top_open, bottom_open)
        done = [jnp.concatenate([x[HALO : 2 * HALO, :width], x[n_rows : n_rows + HALO, :width]], axis=0) for x in done]
        h_ref[:, pl.ds(start, width)] = done[0]
        return done

    over_pieces(at_ref, n_cols, outs, work)


def forecast(kernel, name, at, arrays, n_rows, n_cols, count, extra=()):
    shapes = [(3, n_rows, n_cols // count)] * count + [(n_rows, n_cols)] + list(extra)
    outs = pl.pallas_call(
        kernel,
        out_shape=[jax.ShapeDtypeStruct(shape, jnp.float32) for shape in shapes],
        in_specs=[in_smem] + [in_vmem] * len(arrays),
        out_specs=[in_vmem] * len(shapes),
        compiler_params=pltpu.CompilerParams(vmem_limit_bytes=VMEM_BYTES),
        name=name,
    )(at, *arrays)
    return list(outs[:count]), outs[count:]


def misfit_kernel(at_ref, index_ref, value_ref, var_ref, inner_ref, outer_ref, out_ref, total_ref):
    inner_rows, n_cols = inner_ref.shape
    n_rows = inner_rows + 2 * HALO
    base = at_ref[3] * (n_rows * n_cols)
    row_in = lax.broadcasted_iota(jnp.int32, (8, LANES), 0)
    lane_in = lax.broadcasted_iota(jnp.int32, (8, LANES), 1)

    def tile(ref, row, col):
        first_row = pl.multiple_of(jnp.bitwise_and(row, -8), 8)
        first_col = pl.multiple_of(jnp.bitwise_and(col, -LANES), LANES)
        return ref[pl.ds(first_row, 8), pl.ds(first_col, LANES)]

    def point(k, carry):
        offset = index_ref[k] - base

        @pl.when(jnp.logical_and(offset >= 0, offset < n_rows * n_cols))
        def _():
            row = lax.div(offset, n_cols)
            col = offset - row * n_cols
            inner_row = row - HALO
            is_inner = jnp.logical_and(inner_row >= 0, inner_row < inner_rows)
            outer_row = jnp.where(row < HALO, row, row - inner_rows)
            hit = (row_in == jnp.bitwise_and(row, 7)) & (lane_in == jnp.bitwise_and(col, LANES - 1))

            def add(seen):
                total_ref[...] += jnp.where(hit, (value_ref[k] - seen) ** 2 / var_ref[k], 0.0)

            @pl.when(is_inner)
            def _():
                add(tile(inner_ref, inner_row, col))

            @pl.when(jnp.logical_not(is_inner))
            def _():
                add(tile(outer_ref, outer_row, col))

        return carry

    total_ref[...] = jnp.zeros_like(total_ref)
    lax.fori_loop(0, index_ref.shape[0], point, 0)
    out_ref[...] = jnp.broadcast_to(jnp.sum(total_ref[...]), out_ref.shape)


def misfit(at, obs_index, obs_value, obs_var, inner, outer):
    return pl.pallas_call(
        misfit_kernel,
        out_shape=jax.ShapeDtypeStruct((8, LANES), jnp.float32),
        in_specs=[in_smem] * 4 + [in_vmem] * 2,
        out_specs=in_vmem,
        scratch_shapes=[pltpu.VMEM((8, LANES), jnp.float32)],
        compiler_params=pltpu.CompilerParams(vmem_limit_bytes=VMEM_BYTES),
        name="misfit",
    )(at, obs_index, obs_value, obs_var, inner, outer)[0, 0]


def sum_over(x, axis):
    count = lax.axis_size(axis)
    step = 1
    while step < count:
        x = x + lax.ppermute(x, axis, [(i, i ^ step) for i in range(count)])
        step *= 2
    return x


def log_weight(misfit_sum):
    loglik = sum_over(-0.5 * misfit_sum, "rows")
    slots = lax.broadcasted_iota(jnp.int32, (lax.axis_size("dom"),), 0)
    every = sum_over(jnp.where(slots == lax.axis_index("dom"), loglik, 0.0), "dom")
    peak = jnp.max(every)
    total = jnp.sum(jnp.exp(every - peak))
    return (loglik - (peak + jnp.log(total)))[None]


def place(at, pieces, spans, shape, into=None):
    count = len(pieces)
    n_cols = shape[-1]
    width = n_cols // count

    def kernel(at_ref, *refs):
        srcs = refs[:count]
        dst, sems = refs[-2], refs[-1]
        copies = []
        for m in range(count):
            first = pl.multiple_of(jnp.bitwise_xor(at_ref[0], m) * width, LANES)
            for s, (src_row, dst_row, size) in enumerate(spans):
                copies.append(
                    pltpu.make_async_copy(
                        srcs[m].at[:, pl.ds(src_row, size), :],
                        dst.at[0, :, pl.ds(dst_row, size), pl.ds(first, width)],
                        sems.at[m * len(spans) + s],
                    )
                )
        for c in copies:
            c.start()
        for c in copies:
            c.wait()

    extra = [] if into is None else [into]
    return pl.pallas_call(
        kernel,
        out_shape=pltpu.HBM(shape, jnp.float32),
        in_specs=[in_smem] + [in_vmem] * count + [in_hbm] * len(extra),
        out_specs=in_hbm,
        scratch_shapes=[pltpu.SemaphoreType.DMA((count * len(spans),))],
        input_output_aliases={} if into is None else {count + 1: 0},
        compiler_params=pltpu.CompilerParams(vmem_limit_bytes=VMEM_BYTES),
        name="place",
    )(at, *pieces, *extra)


def route_kernel(at_ref, parents_ref, out_ref, *, half):
    own = at_ref[0]
    side = at_ref[4]
    parents = [parents_ref[s] for s in range(2 * half)]

    def ranks(first):
        other = half - first
        running = jnp.int32(0)
        needed, rank = [], []
        for q in range(half):
            hit = jnp.int32(0)
            for s in range(half):
                hit = hit | jnp.where(parents[other + s] == first + q, 1, 0).astype(jnp.int32)
            needed.append(hit)
            rank.append(running)
            running = running + hit
        return needed, rank, running

    low = ranks(0)
    high = ranks(half)
    out_ref[0] = jnp.maximum(low[2], high[2])
    mine = [jnp.where(side == 0, a, b) for a, b in zip(low[0], high[0])]
    my_rank = [jnp.where(side == 0, a, b) for a, b in zip(low[1], high[1])]
    other_rank = [jnp.where(side == 0, b, a) for a, b in zip(low[1], high[1])]
    for k in range(half):
        chosen = jnp.int32(0)
        for q in range(half):
            chosen = jnp.where((mine[q] == 1) & (my_rank[q] == k), q, chosen)
        out_ref[1 + k] = jnp.bitwise_xor(chosen, own)
    for m in range(half):
        slot = jnp.bitwise_xor(own, m)
        parent = jnp.int32(0)
        for s in range(half):
            parent = jnp.where(slot == s, jnp.where(side == 0, parents[s], parents[half + s]), parent)
        local = parent - side * half
        remote = parent - (1 - side) * half
        from_rank = jnp.int32(0)
        for q in range(half):
            from_rank = jnp.where(remote == q, other_rank[q], from_rank)
        is_local = jnp.logical_and(local >= 0, local < half)
        out_ref[1 + half + m] = jnp.where(is_local, jnp.bitwise_xor(local, own), half + from_rank)


def route(at, parent_lookup, half):
    return pl.pallas_call(
        lambda *refs: route_kernel(*refs, half=half),
        out_shape=jax.ShapeDtypeStruct((1 + 2 * half,), jnp.int32),
        in_specs=[in_smem, in_smem],
        out_specs=in_smem,
        name="route",
    )(at, parent_lookup)


def to_mate(x, m):
    return lax.ppermute(x, "dom", [(i, i ^ m) for i in range(lax.axis_size("dom"))])


def among_mates(pieces):
    return [x if m == 0 else to_mate(x, m) for m, x in enumerate(pieces)]


def chosen(held, routes, crossing):
    return [lax.select_n(routes[1 + k], *held) for k in range(crossing)]


def across(pieces, half):
    return [to_mate(x, half) for x in pieces]


def for_slots(held, got, routes):
    half = len(held)
    return [lax.select_n(routes[1 + half + m], *held, *got) for m in range(half)]


def after(x, *earlier):
    return lax.optimization_barrier((x, earlier))[0]


def halo_rows(head, tail):
    count = lax.axis_size("rows")
    above = lax.ppermute(tail, "rows", [(i, i + 1) for i in range(count - 1)])
    below = lax.ppermute(head, "rows", [(i + 1, i) for i in range(count - 1)])
    return above, below


def inner_forecast(at, fields, depth, count):
    n_rows, n_cols = depth.shape
    rim = (4, HALO, n_cols)
    return forecast(inner_kernel, "inner", at, (fields, depth), n_rows - 2 * HALO, n_cols, count, (rim, rim))


def outer_forecast(at, fields, depth, above, below, count):
    return forecast(outer_kernel, "outer", at, (fields, depth, above, below), 2 * HALO, depth.shape[1], count)


def cycle(crossing, routes, at, fields, depth, obs_index, obs_value, obs_var):
    half = lax.axis_size("dom") // 2
    n_rows, n_cols = depth.shape
    inner, (inner_h, head, tail) = inner_forecast(at, fields, depth, half)
    inner_held = among_mates(inner)
    above, below = halo_rows(head, tail)
    inner_chosen = chosen(inner_held, routes, crossing)
    inner_got = across(inner_chosen, half)
    outer, (outer_h,) = outer_forecast(at, fields, depth, above, after(below, inner_chosen), half)
    outer_held = among_mates(outer)
    outer_chosen = chosen(outer_held, routes, crossing)
    outer_got = across(outer_chosen, half)
    log_weights = log_weight(misfit(at, obs_index, obs_value, obs_var, inner_h, after(outer_h, outer_chosen)))
    inner_done = among_mates(for_slots(inner_held, after(inner_got, outer), routes))
    outer_done = among_mates(for_slots(outer_held, outer_got, routes))
    members = place(at, inner_done, ((0, HALO, n_rows - 2 * HALO),), fields.shape)
    members = place(at, outer_done, ((0, 0, HALO), (HALO, n_rows - HALO, HALO)), fields.shape, members)
    return log_weights, members


def shards(fields, depth, obs_index, obs_value, obs_var, parent_lookup):
    rows_at = lax.axis_index("rows")
    dom_at = lax.axis_index("dom")
    half = lax.axis_size("dom") // 2
    at = jnp.stack(
        [dom_at % half, rows_at > 0, rows_at < lax.axis_size("rows") - 1, rows_at, dom_at // half]
    ).astype(jnp.int32)
    if half == 4:
        routes = route(at, parent_lookup, half)
        branches = [
            (lambda r, a, *rest, c=c: cycle(c, r, a, *rest)) for c in range(1, half + 1)
        ]
        return lax.switch(
            jnp.clip(routes[0] - 1, 0, half - 1), branches, routes, at, fields, depth, obs_index, obs_value, obs_var
        )
    return by_pieces(at, fields, depth, obs_index, obs_value, obs_var, parent_lookup)


def by_pieces(at, fields, depth, obs_index, obs_value, obs_var, parent_lookup):
    pieces = lax.axis_size("dom")
    n_rows, n_cols = depth.shape
    whole = at * jnp.array([0, 1, 1, 1, 1], jnp.int32)
    (inner,), (inner_h, head, tail) = inner_forecast(whole, fields, depth, 1)
    (outer,), (outer_h,) = outer_forecast(whole, fields, depth, *halo_rows(head, tail), 1)
    log_weights = log_weight(misfit(at, obs_index, obs_value, obs_var, inner_h, outer_h))
    slab = jnp.concatenate([outer[:, :HALO], inner, outer[:, HALO:]], axis=1)
    tiles = slab.reshape(3, n_rows, pieces, n_cols // pieces).transpose(2, 0, 1, 3)
    received = lax.all_to_all(tiles, "dom", split_axis=0, concat_axis=0, tiled=True)
    picked = jnp.take(received, parent_lookup, axis=0, mode="clip")
    final = lax.all_to_all(picked, "dom", split_axis=0, concat_axis=0, tiled=True)
    return log_weights, final.transpose(1, 2, 0, 3).reshape(1, 3, n_rows, n_cols)


def solution(mesh):
    in_specs = (P("dom", None, "rows", None), P("rows", None), P(), P(), P(), P())
    out_specs = (P("dom"), P("dom", None, "rows", None))
    return jax.shard_map(shards, mesh=mesh, in_specs=in_specs, out_specs=out_specs, check_vma=False)
```

```python
import jax
import jax.numpy as jnp
from jax import lax
from jax.experimental import pallas as pl
from jax.experimental.pallas import tpu as pltpu
from jax.sharding import PartitionSpec as P

STEPS = 4
HALO = 2 * STEPS
LANES = 128
VMEM_BYTES = 48 * 2**20

time_step = 0.5
coriolis = 0.2

in_vmem = pl.BlockSpec(memory_space=pltpu.VMEM)
in_smem = pl.BlockSpec(memory_space=pltpu.SMEM)
in_hbm = pl.BlockSpec(memory_space=pltpu.HBM)


def model_steps(h_ref, u_ref, v_ref, d_ref, top_open=None, bottom_open=None):
    n_rows, n_cols = h_ref.shape
    h_ref[...] = h_ref[...] * (0.5 * time_step)
    d_ref[...] = d_ref[...] * (0.25 * time_step * time_step)

    def cols(a):
        return pltpu.roll(a, n_cols - 1, 1) - pltpu.roll(a, 1, 1)

    def rows(a):
        return pltpu.roll(a, n_rows - 1, 0) - pltpu.roll(a, 1, 0)

    def step(_, carry):
        u = u_ref[...]
        v = v_ref[...]
        d = d_ref[...]
        h = h_ref[...] - (cols(d * u) + rows(d * v))
        if top_open is not None:
            h = jnp.concatenate(
                [h[:HALO] * top_open, h[HALO : n_rows - HALO], h[n_rows - HALO :] * bottom_open], axis=0
            )
        h_ref[...] = h
        u = u - cols(h) + (time_step * coriolis) * v
        u_ref[...] = u
        v_ref[...] = v - rows(h) - (time_step * coriolis) * u
        return carry

    lax.fori_loop(0, STEPS, step, 0)
    h_ref[...] = h_ref[...] * (2.0 / time_step)


def store_pieces(at_ref, outs, state, rows_of):
    width = outs[0].shape[-1]
    for m, out in enumerate(outs):
        start = pl.multiple_of(jnp.bitwise_xor(at_ref[0], m) * width, LANES)
        for k, ref in enumerate(state[:3]):
            out[k] = rows_of(ref, pl.ds(start, width))


def inner_kernel(at_ref, fields_ref, depth_ref, *refs):
    outs, (h_ref, head_ref, tail_ref), state = refs[:-7], refs[-7:-4], refs[-4:]
    n_rows = depth_ref.shape[0]
    for k in range(4):
        field = depth_ref[...] if k == 3 else fields_ref[0, k]
        state[k][...] = field
        head_ref[k] = field[:HALO]
        tail_ref[k] = field[n_rows - HALO :]
    model_steps(*state)
    h_ref[...] = state[0][HALO : n_rows - HALO]
    store_pieces(at_ref, outs, state, lambda ref, at: ref[HALO : n_rows - HALO, at])


def outer_kernel(at_ref, fields_ref, depth_ref, above_ref, below_ref, *refs):
    outs, h_ref, state = refs[:-5], refs[-5], refs[-4:]
    n_rows = depth_ref.shape[0]
    for k in range(4):
        state[k][:HALO] = above_ref[k]
        state[k][HALO : HALO + n_rows] = depth_ref[...] if k == 3 else fields_ref[0, k]
        state[k][HALO + n_rows :] = below_ref[k]
    model_steps(*state, at_ref[1].astype(jnp.float32), at_ref[2].astype(jnp.float32))

    def outer_rows(ref, at):
        return jnp.concatenate([ref[HALO : 2 * HALO, at], ref[n_rows : n_rows + HALO, at]], axis=0)

    h_ref[...] = outer_rows(state[0], pl.ds(0, depth_ref.shape[1]))
    store_pieces(at_ref, outs, state, outer_rows)


def forecast(kernel, name, at, arrays, n_rows, n_cols, count, window_rows, extra=()):
    shapes = [(3, n_rows, n_cols // count)] * count + [(n_rows, n_cols)] + list(extra)
    outs = pl.pallas_call(
        kernel,
        out_shape=[jax.ShapeDtypeStruct(shape, jnp.float32) for shape in shapes],
        in_specs=[in_smem] + [in_vmem] * len(arrays),
        out_specs=[in_vmem] * len(shapes),
        scratch_shapes=[pltpu.VMEM((window_rows, n_cols), jnp.float32)] * 4,
        compiler_params=pltpu.CompilerParams(vmem_limit_bytes=VMEM_BYTES),
        name=name,
    )(at, *arrays)
    return list(outs[:count]), outs[count:]


def misfit_kernel(at_ref, index_ref, value_ref, var_ref, inner_ref, outer_ref, out_ref, total_ref):
    inner_rows, n_cols = inner_ref.shape
    n_rows = inner_rows + 2 * HALO
    base = at_ref[3] * (n_rows * n_cols)
    row_in = lax.broadcasted_iota(jnp.int32, (8, LANES), 0)
    lane_in = lax.broadcasted_iota(jnp.int32, (8, LANES), 1)

    def tile(ref, row, col):
        first_row = pl.multiple_of(jnp.bitwise_and(row, -8), 8)
        first_col = pl.multiple_of(jnp.bitwise_and(col, -LANES), LANES)
        return ref[pl.ds(first_row, 8), pl.ds(first_col, LANES)]

    def point(k, carry):
        offset = index_ref[k] - base

        @pl.when(jnp.logical_and(offset >= 0, offset < n_rows * n_cols))
        def _():
            row = lax.div(offset, n_cols)
            col = offset - row * n_cols
            inner_row = row - HALO
            is_inner = jnp.logical_and(inner_row >= 0, inner_row < inner_rows)
            outer_row = jnp.where(row < HALO, row, row - inner_rows)
            hit = (row_in == jnp.bitwise_and(row, 7)) & (lane_in == jnp.bitwise_and(col, LANES - 1))

            def add(seen):
                total_ref[...] += jnp.where(hit, (value_ref[k] - seen) ** 2 / var_ref[k], 0.0)

            @pl.when(is_inner)
            def _():
                add(tile(inner_ref, inner_row, col))

            @pl.when(jnp.logical_not(is_inner))
            def _():
                add(tile(outer_ref, outer_row, col))

        return carry

    total_ref[...] = jnp.zeros_like(total_ref)
    lax.fori_loop(0, index_ref.shape[0], point, 0)
    out_ref[...] = jnp.broadcast_to(jnp.sum(total_ref[...]), out_ref.shape)


def misfit(at, obs_index, obs_value, obs_var, inner, outer):
    return pl.pallas_call(
        misfit_kernel,
        out_shape=jax.ShapeDtypeStruct((8, LANES), jnp.float32),
        in_specs=[in_smem] * 4 + [in_vmem] * 2,
        out_specs=in_vmem,
        scratch_shapes=[pltpu.VMEM((8, LANES), jnp.float32)],
        compiler_params=pltpu.CompilerParams(vmem_limit_bytes=VMEM_BYTES),
        name="misfit",
    )(at, obs_index, obs_value, obs_var, inner, outer)[0, 0]


def sum_over(x, axis):
    count = lax.axis_size(axis)
    step = 1
    while step < count:
        x = x + lax.ppermute(x, axis, [(i, i ^ step) for i in range(count)])
        step *= 2
    return x


def log_weight(misfit_sum):
    loglik = sum_over(-0.5 * misfit_sum, "rows")
    slots = lax.broadcasted_iota(jnp.int32, (lax.axis_size("dom"),), 0)
    every = sum_over(jnp.where(slots == lax.axis_index("dom"), loglik, 0.0), "dom")
    peak = jnp.max(every)
    total = jnp.sum(jnp.exp(every - peak))
    return (loglik - (peak + jnp.log(total)))[None]


def place(at, pieces, spans, shape, into=None):
    count = len(pieces)
    n_cols = shape[-1]
    width = n_cols // count

    def kernel(at_ref, *refs):
        srcs = refs[:count]
        dst, sems = refs[-2], refs[-1]
        copies = []
        for m in range(count):
            first = pl.multiple_of(jnp.bitwise_xor(at_ref[0], m) * width, LANES)
            for s, (src_row, dst_row, size) in enumerate(spans):
                copies.append(
                    pltpu.make_async_copy(
                        srcs[m].at[:, pl.ds(src_row, size), :],
                        dst.at[0, :, pl.ds(dst_row, size), pl.ds(first, width)],
                        sems.at[m * len(spans) + s],
                    )
                )
        for c in copies:
            c.start()
        for c in copies:
            c.wait()

    extra = [] if into is None else [into]
    return pl.pallas_call(
        kernel,
        out_shape=pltpu.HBM(shape, jnp.float32),
        in_specs=[in_smem] + [in_vmem] * count + [in_hbm] * len(extra),
        out_specs=in_hbm,
        scratch_shapes=[pltpu.SemaphoreType.DMA((count * len(spans),))],
        input_output_aliases={} if into is None else {count + 1: 0},
        compiler_params=pltpu.CompilerParams(vmem_limit_bytes=VMEM_BYTES),
        name="place",
    )(at, *pieces, *extra)


def route_kernel(at_ref, parents_ref, out_ref, *, half):
    own = at_ref[0]
    side = at_ref[4]
    parents = [parents_ref[s] for s in range(2 * half)]

    def ranks(first):
        other = half - first
        running = jnp.int32(0)
        needed, rank = [], []
        for q in range(half):
            hit = jnp.int32(0)
            for s in range(half):
                hit = hit | jnp.where(parents[other + s] == first + q, 1, 0).astype(jnp.int32)
            needed.append(hit)
            rank.append(running)
            running = running + hit
        return needed, rank, running

    low = ranks(0)
    high = ranks(half)
    out_ref[0] = jnp.maximum(low[2], high[2])
    mine = [jnp.where(side == 0, a, b) for a, b in zip(low[0], high[0])]
    my_rank = [jnp.where(side == 0, a, b) for a, b in zip(low[1], high[1])]
    other_rank = [jnp.where(side == 0, b, a) for a, b in zip(low[1], high[1])]
    for k in range(half):
        chosen = jnp.int32(0)
        for q in range(half):
            chosen = jnp.where((mine[q] == 1) & (my_rank[q] == k), q, chosen)
        out_ref[1 + k] = jnp.bitwise_xor(chosen, own)
    for m in range(half):
        slot = jnp.bitwise_xor(own, m)
        parent = jnp.int32(0)
        for s in range(half):
            parent = jnp.where(slot == s, jnp.where(side == 0, parents[s], parents[half + s]), parent)
        local = parent - side * half
        remote = parent - (1 - side) * half
        from_rank = jnp.int32(0)
        for q in range(half):
            from_rank = jnp.where(remote == q, other_rank[q], from_rank)
        is_local = jnp.logical_and(local >= 0, local < half)
        out_ref[1 + half + m] = jnp.where(is_local, jnp.bitwise_xor(local, own), half + from_rank)


def route(at, parent_lookup, half):
    return pl.pallas_call(
        lambda *refs: route_kernel(*refs, half=half),
        out_shape=jax.ShapeDtypeStruct((1 + 2 * half,), jnp.int32),
        in_specs=[in_smem, in_smem],
        out_specs=in_smem,
        name="route",
    )(at, parent_lookup)


def to_mate(x, m):
    return lax.ppermute(x, "dom", [(i, i ^ m) for i in range(lax.axis_size("dom"))])


def among_mates(pieces):
    return [x if m == 0 else to_mate(x, m) for m, x in enumerate(pieces)]


def pick(routes, first, sources, count):
    def kernel(routes_ref, *refs):
        srcs, outs = refs[: len(sources)], refs[len(sources) :]
        for m, out in enumerate(outs):
            which = routes_ref[first + m]
            for s, src in enumerate(srcs):

                @pl.when(which == s)
                def _(src=src, out=out):
                    out[...] = src[...]

    return pl.pallas_call(
        kernel,
        out_shape=[jax.ShapeDtypeStruct(sources[0].shape, jnp.float32)] * count,
        in_specs=[in_smem] + [in_vmem] * len(sources),
        out_specs=[in_vmem] * count,
        compiler_params=pltpu.CompilerParams(vmem_limit_bytes=VMEM_BYTES),
        name="pick",
    )(routes, *sources)


def chosen(held, routes, crossing):
    return pick(routes, 1, held, crossing)


def across(pieces, half):
    return [to_mate(x, half) for x in pieces]


def for_slots(held, got, routes):
    return pick(routes, 1 + len(held), [*held, *got], len(held))


def after(x, *earlier):
    return lax.optimization_barrier((x, earlier))[0]


def halo_rows(head, tail):
    count = lax.axis_size("rows")
    above = lax.ppermute(tail, "rows", [(i, i + 1) for i in range(count - 1)])
    below = lax.ppermute(head, "rows", [(i + 1, i) for i in range(count - 1)])
    return above, below


def inner_forecast(at, fields, depth, count):
    n_rows, n_cols = depth.shape
    rim = (4, HALO, n_cols)
    return forecast(inner_kernel, "inner", at, (fields, depth), n_rows - 2 * HALO, n_cols, count, n_rows, (rim, rim))


def outer_forecast(at, fields, depth, above, below, count):
    n_rows, n_cols = depth.shape
    arrays = (fields, depth, above, below)
    return forecast(outer_kernel, "outer", at, arrays, 2 * HALO, n_cols, count, n_rows + 2 * HALO)


def cycle(crossing, routes, at, fields, depth, obs_index, obs_value, obs_var):
    half = lax.axis_size("dom") // 2
    n_rows, n_cols = depth.shape
    inner, (inner_h, head, tail) = inner_forecast(at, fields, depth, half)
    inner_held = among_mates(inner)
    above, below = halo_rows(head, tail)
    inner_chosen = chosen(inner_held, routes, crossing)
    inner_got = across(inner_chosen, half)
    outer, (outer_h,) = outer_forecast(at, fields, depth, above, after(below, inner_chosen), half)
    outer_held = among_mates(outer)
    outer_chosen = chosen(outer_held, routes, crossing)
    outer_got = across(outer_chosen, half)
    log_weights = log_weight(after(misfit(at, obs_index, obs_value, obs_var, inner_h, outer_h), outer_chosen))
    inner_done = among_mates(for_slots(inner_held, after(inner_got, outer), routes))
    outer_done = among_mates(for_slots(outer_held, outer_got, routes))
    members = place(at, inner_done, ((0, HALO, n_rows - 2 * HALO),), fields.shape)
    members = place(at, outer_done, ((0, 0, HALO), (HALO, n_rows - HALO, HALO)), fields.shape, members)
    return log_weights, members


def shards(fields, depth, obs_index, obs_value, obs_var, parent_lookup):
    rows_at = lax.axis_index("rows")
    dom_at = lax.axis_index("dom")
    half = lax.axis_size("dom") // 2
    at = jnp.stack(
        [dom_at % half, rows_at > 0, rows_at < lax.axis_size("rows") - 1, rows_at, dom_at // half]
    ).astype(jnp.int32)
    if half == 4:
        routes = route(at, parent_lookup, half)
        branches = [
            (lambda r, a, *rest, c=c: cycle(c, r, a, *rest)) for c in range(1, half + 1)
        ]
        return lax.switch(
            jnp.clip(routes[0] - 1, 0, half - 1), branches, routes, at, fields, depth, obs_index, obs_value, obs_var
        )
    return by_pieces(at, fields, depth, obs_index, obs_value, obs_var, parent_lookup)


def by_pieces(at, fields, depth, obs_index, obs_value, obs_var, parent_lookup):
    pieces = lax.axis_size("dom")
    n_rows, n_cols = depth.shape
    whole = at * jnp.array([0, 1, 1, 1, 1], jnp.int32)
    (inner,), (inner_h, head, tail) = inner_forecast(whole, fields, depth, 1)
    (outer,), (outer_h,) = outer_forecast(whole, fields, depth, *halo_rows(head, tail), 1)
    log_weights = log_weight(misfit(at, obs_index, obs_value, obs_var, inner_h, outer_h))
    slab = jnp.concatenate([outer[:, :HALO], inner, outer[:, HALO:]], axis=1)
    tiles = slab.reshape(3, n_rows, pieces, n_cols // pieces).transpose(2, 0, 1, 3)
    received = lax.all_to_all(tiles, "dom", split_axis=0, concat_axis=0, tiled=True)
    picked = jnp.take(received, parent_lookup, axis=0, mode="clip")
    final = lax.all_to_all(picked, "dom", split_axis=0, concat_axis=0, tiled=True)
    return log_weights, final.transpose(1, 2, 0, 3).reshape(1, 3, n_rows, n_cols)


def solution(mesh):
    in_specs = (P("dom", None, "rows", None), P("rows", None), P(), P(), P(), P())
    out_specs = (P("dom"), P("dom", None, "rows", None))
    return jax.shard_map(shards, mesh=mesh, in_specs=in_specs, out_specs=out_specs, check_vma=False)
```

```python
import jax
import jax.numpy as jnp
from jax import lax
from jax.experimental import pallas as pl
from jax.experimental.pallas import tpu as pltpu
from jax.sharding import PartitionSpec as P

STEPS = 4
HALO = 2 * STEPS
LANES = 128
VMEM_BYTES = 48 * 2**20

time_step = 0.5
coriolis = 0.2

in_vmem = pl.BlockSpec(memory_space=pltpu.VMEM)
in_smem = pl.BlockSpec(memory_space=pltpu.SMEM)
in_hbm = pl.BlockSpec(memory_space=pltpu.HBM)


def model_steps(h_ref, u_ref, v_ref, d_ref, top_open=None, bottom_open=None):
    n_rows, n_cols = h_ref.shape
    h_ref[...] = h_ref[...] * (0.5 * time_step)
    d_ref[...] = d_ref[...] * (0.25 * time_step * time_step)

    def cols(a):
        return pltpu.roll(a, n_cols - 1, 1) - pltpu.roll(a, 1, 1)

    def rows(a):
        return pltpu.roll(a, n_rows - 1, 0) - pltpu.roll(a, 1, 0)

    def step(_, carry):
        u = u_ref[...]
        v = v_ref[...]
        d = d_ref[...]
        h = h_ref[...] - (cols(d * u) + rows(d * v))
        if top_open is not None:
            h = jnp.concatenate(
                [h[:HALO] * top_open, h[HALO : n_rows - HALO], h[n_rows - HALO :] * bottom_open], axis=0
            )
        h_ref[...] = h
        u = u - cols(h) + (time_step * coriolis) * v
        u_ref[...] = u
        v_ref[...] = v - rows(h) - (time_step * coriolis) * u
        return carry

    lax.fori_loop(0, STEPS, step, 0)
    h_ref[...] = h_ref[...] * (2.0 / time_step)


def store_pieces(at_ref, outs, state, rows_of):
    width = outs[0].shape[-1]
    for m, out in enumerate(outs):
        start = pl.multiple_of(jnp.bitwise_xor(at_ref[0], m) * width, LANES)
        for k, ref in enumerate(state[:3]):
            out[k] = rows_of(ref, pl.ds(start, width))


def inner_kernel(at_ref, fields_ref, depth_ref, *refs):
    outs, (h_ref, head_ref, tail_ref), state = refs[:-7], refs[-7:-4], refs[-4:]
    n_rows = depth_ref.shape[0]
    for k in range(4):
        field = depth_ref[...] if k == 3 else fields_ref[0, k]
        state[k][...] = field
        head_ref[k] = field[:HALO]
        tail_ref[k] = field[n_rows - HALO :]
    model_steps(*state)
    h_ref[...] = state[0][HALO : n_rows - HALO]
    store_pieces(at_ref, outs, state, lambda ref, at: ref[HALO : n_rows - HALO, at])


def outer_kernel(at_ref, fields_ref, depth_ref, above_ref, below_ref, *refs):
    outs, h_ref, state = refs[:-5], refs[-5], refs[-4:]
    n_rows = depth_ref.shape[0]
    for k in range(4):
        state[k][:HALO] = above_ref[k]
        state[k][HALO : HALO + n_rows] = depth_ref[...] if k == 3 else fields_ref[0, k]
        state[k][HALO + n_rows :] = below_ref[k]
    model_steps(*state, at_ref[1].astype(jnp.float32), at_ref[2].astype(jnp.float32))

    def outer_rows(ref, at):
        return jnp.concatenate([ref[HALO : 2 * HALO, at], ref[n_rows : n_rows + HALO, at]], axis=0)

    h_ref[...] = outer_rows(state[0], pl.ds(0, depth_ref.shape[1]))
    store_pieces(at_ref, outs, state, outer_rows)


def forecast(kernel, name, at, arrays, n_rows, n_cols, count, window_rows, extra=()):
    shapes = [(3, n_rows, n_cols // count)] * count + [(n_rows, n_cols)] + list(extra)
    outs = pl.pallas_call(
        kernel,
        out_shape=[jax.ShapeDtypeStruct(shape, jnp.float32) for shape in shapes],
        in_specs=[in_smem] + [in_vmem] * len(arrays),
        out_specs=[in_vmem] * len(shapes),
        scratch_shapes=[pltpu.VMEM((window_rows, n_cols), jnp.float32)] * 4,
        compiler_params=pltpu.CompilerParams(vmem_limit_bytes=VMEM_BYTES),
        name=name,
    )(at, *arrays)
    return list(outs[:count]), outs[count:]


def misfit_kernel(at_ref, index_ref, value_ref, var_ref, inner_ref, outer_ref, out_ref, total_ref):
    inner_rows, n_cols = inner_ref.shape
    n_rows = inner_rows + 2 * HALO
    base = at_ref[3] * (n_rows * n_cols)
    row_in = lax.broadcasted_iota(jnp.int32, (8, LANES), 0)
    lane_in = lax.broadcasted_iota(jnp.int32, (8, LANES), 1)

    def tile(ref, row, col):
        first_row = pl.multiple_of(jnp.bitwise_and(row, -8), 8)
        first_col = pl.multiple_of(jnp.bitwise_and(col, -LANES), LANES)
        return ref[pl.ds(first_row, 8), pl.ds(first_col, LANES)]

    def point(k, carry):
        offset = index_ref[k] - base

        @pl.when(jnp.logical_and(offset >= 0, offset < n_rows * n_cols))
        def _():
            row = lax.div(offset, n_cols)
            col = offset - row * n_cols
            inner_row = row - HALO
            is_inner = jnp.logical_and(inner_row >= 0, inner_row < inner_rows)
            outer_row = jnp.where(row < HALO, row, row - inner_rows)
            hit = (row_in == jnp.bitwise_and(row, 7)) & (lane_in == jnp.bitwise_and(col, LANES - 1))

            def add(seen):
                total_ref[...] += jnp.where(hit, (value_ref[k] - seen) ** 2 / var_ref[k], 0.0)

            @pl.when(is_inner)
            def _():
                add(tile(inner_ref, inner_row, col))

            @pl.when(jnp.logical_not(is_inner))
            def _():
                add(tile(outer_ref, outer_row, col))

        return carry

    total_ref[...] = jnp.zeros_like(total_ref)
    lax.fori_loop(0, index_ref.shape[0], point, 0, unroll=8)
    out_ref[...] = jnp.broadcast_to(jnp.sum(total_ref[...]), out_ref.shape)


def misfit(at, obs_index, obs_value, obs_var, inner, outer):
    return pl.pallas_call(
        misfit_kernel,
        out_shape=jax.ShapeDtypeStruct((8, LANES), jnp.float32),
        in_specs=[in_smem] * 4 + [in_vmem] * 2,
        out_specs=in_vmem,
        scratch_shapes=[pltpu.VMEM((8, LANES), jnp.float32)],
        compiler_params=pltpu.CompilerParams(vmem_limit_bytes=VMEM_BYTES),
        name="misfit",
    )(at, obs_index, obs_value, obs_var, inner, outer)[0, 0]


def sum_over(x, axis):
    count = lax.axis_size(axis)
    step = 1
    while step < count:
        x = x + lax.ppermute(x, axis, [(i, i ^ step) for i in range(count)])
        step *= 2
    return x


def log_weight(loglik):
    slots = lax.broadcasted_iota(jnp.int32, (lax.axis_size("dom"),), 0)
    every = sum_over(jnp.where(slots == lax.axis_index("dom"), loglik, 0.0), "dom")
    peak = jnp.max(every)
    total = jnp.sum(jnp.exp(every - peak))
    return (loglik - (peak + jnp.log(total)))[None]


def place(at, pieces, spans, shape, into=None):
    count = len(pieces)
    n_cols = shape[-1]
    width = n_cols // count

    def kernel(at_ref, *refs):
        srcs = refs[:count]
        dst, sems = refs[-2], refs[-1]
        copies = []
        for m in range(count):
            first = pl.multiple_of(jnp.bitwise_xor(at_ref[0], m) * width, LANES)
            for s, (src_row, dst_row, size) in enumerate(spans):
                copies.append(
                    pltpu.make_async_copy(
                        srcs[m].at[:, pl.ds(src_row, size), :],
                        dst.at[0, :, pl.ds(dst_row, size), pl.ds(first, width)],
                        sems.at[m * len(spans) + s],
                    )
                )
        for c in copies:
            c.start()
        for c in copies:
            c.wait()

    extra = [] if into is None else [into]
    return pl.pallas_call(
        kernel,
        out_shape=pltpu.HBM(shape, jnp.float32),
        in_specs=[in_smem] + [in_vmem] * count + [in_hbm] * len(extra),
        out_specs=in_hbm,
        scratch_shapes=[pltpu.SemaphoreType.DMA((count * len(spans),))],
        input_output_aliases={} if into is None else {count + 1: 0},
        compiler_params=pltpu.CompilerParams(vmem_limit_bytes=VMEM_BYTES),
        name="place",
    )(at, *pieces, *extra)


def route_kernel(at_ref, parents_ref, out_ref, *, half):
    own = at_ref[0]
    side = at_ref[4]
    parents = [parents_ref[s] for s in range(2 * half)]

    def ranks(first):
        other = half - first
        running = jnp.int32(0)
        needed, rank = [], []
        for q in range(half):
            hit = jnp.int32(0)
            for s in range(half):
                hit = hit | jnp.where(parents[other + s] == first + q, 1, 0).astype(jnp.int32)
            needed.append(hit)
            rank.append(running)
            running = running + hit
        return needed, rank, running

    low = ranks(0)
    high = ranks(half)
    out_ref[0] = jnp.maximum(low[2], high[2])
    mine = [jnp.where(side == 0, a, b) for a, b in zip(low[0], high[0])]
    my_rank = [jnp.where(side == 0, a, b) for a, b in zip(low[1], high[1])]
    other_rank = [jnp.where(side == 0, b, a) for a, b in zip(low[1], high[1])]
    for k in range(half):
        chosen = jnp.int32(0)
        for q in range(half):
            chosen = jnp.where((mine[q] == 1) & (my_rank[q] == k), q, chosen)
        out_ref[1 + k] = jnp.bitwise_xor(chosen, own)
    for m in range(half):
        slot = jnp.bitwise_xor(own, m)
        parent = jnp.int32(0)
        for s in range(half):
            parent = jnp.where(slot == s, jnp.where(side == 0, parents[s], parents[half + s]), parent)
        local = parent - side * half
        remote = parent - (1 - side) * half
        from_rank = jnp.int32(0)
        for q in range(half):
            from_rank = jnp.where(remote == q, other_rank[q], from_rank)
        is_local = jnp.logical_and(local >= 0, local < half)
        out_ref[1 + half + m] = jnp.where(is_local, jnp.bitwise_xor(local, own), half + from_rank)


def route(at, parent_lookup, half):
    return pl.pallas_call(
        lambda *refs: route_kernel(*refs, half=half),
        out_shape=jax.ShapeDtypeStruct((1 + 2 * half,), jnp.int32),
        in_specs=[in_smem, in_smem],
        out_specs=in_smem,
        name="route",
    )(at, parent_lookup)


def to_mate(x, m):
    return lax.ppermute(x, "dom", [(i, i ^ m) for i in range(lax.axis_size("dom"))])


def among_mates(pieces):
    return [x if m == 0 else to_mate(x, m) for m, x in enumerate(pieces)]


def pick(routes, first, count, sources, stacks=(), stacked=False):
    block = sources[0].shape

    def kernel(routes_ref, *refs):
        n_in = len(sources) + len(stacks)
        srcs = [(ref, None) for ref in refs[: len(sources)]]
        srcs += [(ref, k) for ref in refs[len(sources) : n_in] for k in range(ref.shape[0])]
        for m in range(count):
            which = routes_ref[first + m]
            for s, (src, k) in enumerate(srcs):

                @pl.when(which == s)
                def _(m=m, src=src, k=k):
                    value = src[...] if k is None else src[k]
                    if stacked:
                        refs[n_in][m] = value
                    else:
                        refs[n_in + m][...] = value

    shapes = [(count,) + block] if stacked else [block] * count
    return pl.pallas_call(
        kernel,
        out_shape=[jax.ShapeDtypeStruct(shape, jnp.float32) for shape in shapes],
        in_specs=[in_smem] + [in_vmem] * (len(sources) + len(stacks)),
        out_specs=[in_vmem] * len(shapes),
        compiler_params=pltpu.CompilerParams(vmem_limit_bytes=VMEM_BYTES),
        name="pick",
    )(routes, *sources, *stacks)


def chosen(held, routes, crossing):
    return pick(routes, 1, crossing, held, stacked=True)[0]


def for_slots(held, got, routes):
    return pick(routes, 1 + len(held), len(held), held, [got])


def after(x, *earlier):
    return lax.optimization_barrier((x, earlier))[0]


def halo_rows(head, tail):
    count = lax.axis_size("rows")
    above = lax.ppermute(tail, "rows", [(i, i + 1) for i in range(count - 1)])
    below = lax.ppermute(head, "rows", [(i + 1, i) for i in range(count - 1)])
    return above, below


def inner_forecast(at, fields, depth, count):
    n_rows, n_cols = depth.shape
    rim = (4, HALO, n_cols)
    return forecast(inner_kernel, "inner", at, (fields, depth), n_rows - 2 * HALO, n_cols, count, n_rows, (rim, rim))


def outer_forecast(at, fields, depth, above, below, count):
    n_rows, n_cols = depth.shape
    arrays = (fields, depth, above, below)
    return forecast(outer_kernel, "outer", at, arrays, 2 * HALO, n_cols, count, n_rows + 2 * HALO)


def cycle(crossing, routes, at, fields, depth, obs_index, obs_value, obs_var):
    half = lax.axis_size("dom") // 2
    n_rows, n_cols = depth.shape
    inner, (inner_h, head, tail) = inner_forecast(at, fields, depth, half)
    inner_held = among_mates(inner)
    rims = halo_rows(head, tail)
    inner_chosen = chosen(inner_held, routes, crossing)
    inner_got = to_mate(inner_chosen, half)
    above, below = after(rims, inner_chosen)
    outer, (outer_h,) = outer_forecast(at, fields, depth, above, below, half)
    outer_held = among_mates(outer)
    misfit_sum = misfit(at, obs_index, obs_value, obs_var, inner_h, outer_h)
    outer_chosen = chosen(outer_held, routes, crossing)
    outer_got = to_mate(outer_chosen, half)
    loglik = sum_over(-0.5 * after(misfit_sum, outer_chosen), "rows")
    inner_done = among_mates(for_slots(inner_held, after(inner_got, outer_chosen), routes))
    outer_slots = for_slots(outer_held, outer_got, routes)
    outer_done = among_mates(outer_slots)
    log_weights = log_weight(after(loglik, outer_slots))
    members = place(at, inner_done, ((0, HALO, n_rows - 2 * HALO),), fields.shape)
    members = place(at, outer_done, ((0, 0, HALO), (HALO, n_rows - HALO, HALO)), fields.shape, members)
    return log_weights, members


def shards(fields, depth, obs_index, obs_value, obs_var, parent_lookup):
    rows_at = lax.axis_index("rows")
    dom_at = lax.axis_index("dom")
    half = lax.axis_size("dom") // 2
    at = jnp.stack(
        [dom_at % half, rows_at > 0, rows_at < lax.axis_size("rows") - 1, rows_at, dom_at // half]
    ).astype(jnp.int32)
    if half == 4:
        routes = route(at, parent_lookup, half)
        branches = [
            (lambda r, a, *rest, c=c: cycle(c, r, a, *rest)) for c in range(1, half + 1)
        ]
        return lax.switch(
            jnp.clip(routes[0] - 1, 0, half - 1), branches, routes, at, fields, depth, obs_index, obs_value, obs_var
        )
    return by_pieces(at, fields, depth, obs_index, obs_value, obs_var, parent_lookup)


def by_pieces(at, fields, depth, obs_index, obs_value, obs_var, parent_lookup):
    pieces = lax.axis_size("dom")
    n_rows, n_cols = depth.shape
    whole = at * jnp.array([0, 1, 1, 1, 1], jnp.int32)
    (inner,), (inner_h, head, tail) = inner_forecast(whole, fields, depth, 1)
    (outer,), (outer_h,) = outer_forecast(whole, fields, depth, *halo_rows(head, tail), 1)
    misfit_sum = misfit(at, obs_index, obs_value, obs_var, inner_h, outer_h)
    log_weights = log_weight(sum_over(-0.5 * misfit_sum, "rows"))
    slab = jnp.concatenate([outer[:, :HALO], inner, outer[:, HALO:]], axis=1)
    tiles = slab.reshape(3, n_rows, pieces, n_cols // pieces).transpose(2, 0, 1, 3)
    received = lax.all_to_all(tiles, "dom", split_axis=0, concat_axis=0, tiled=True)
    picked = jnp.take(received, parent_lookup, axis=0, mode="clip")
    final = lax.all_to_all(picked, "dom", split_axis=0, concat_axis=0, tiled=True)
    return log_weights, final.transpose(1, 2, 0, 3).reshape(1, 3, n_rows, n_cols)


def solution(mesh):
    in_specs = (P("dom", None, "rows", None), P("rows", None), P(), P(), P(), P())
    out_specs = (P("dom"), P("dom", None, "rows", None))
    return jax.shard_map(shards, mesh=mesh, in_specs=in_specs, out_specs=out_specs, check_vma=False)
```

```python
import jax
import jax.numpy as jnp
from jax import lax
from jax.experimental import pallas as pl
from jax.experimental.pallas import tpu as pltpu
from jax.sharding import PartitionSpec as P

STEPS = 4
HALO = 2 * STEPS
LANES = 128
VMEM_BYTES = 48 * 2**20

time_step = 0.5
coriolis = 0.2

in_vmem = pl.BlockSpec(memory_space=pltpu.VMEM)
in_smem = pl.BlockSpec(memory_space=pltpu.SMEM)
in_hbm = pl.BlockSpec(memory_space=pltpu.HBM)


def model_steps(h_ref, u_ref, v_ref, d_ref, top_open=None, bottom_open=None):
    n_rows, n_cols = h_ref.shape
    h_ref[...] = h_ref[...] * (0.5 * time_step)
    d_ref[...] = d_ref[...] * (0.25 * time_step * time_step)

    def cols(a):
        return pltpu.roll(a, n_cols - 1, 1) - pltpu.roll(a, 1, 1)

    def rows(a):
        return pltpu.roll(a, n_rows - 1, 0) - pltpu.roll(a, 1, 0)

    def step(_, carry):
        u = u_ref[...]
        v = v_ref[...]
        d = d_ref[...]
        h = h_ref[...] - (cols(d * u) + rows(d * v))
        if top_open is not None:
            h = jnp.concatenate(
                [h[:HALO] * top_open, h[HALO : n_rows - HALO], h[n_rows - HALO :] * bottom_open], axis=0
            )
        h_ref[...] = h
        u = u - cols(h) + (time_step * coriolis) * v
        u_ref[...] = u
        v_ref[...] = v - rows(h) - (time_step * coriolis) * u
        return carry

    lax.fori_loop(0, STEPS, step, 0)
    h_ref[...] = h_ref[...] * (2.0 / time_step)


def store_pieces(at_ref, outs, state, rows_of):
    width = outs[0].shape[-1]
    for m, out in enumerate(outs):
        start = pl.multiple_of(jnp.bitwise_xor(at_ref[0], m) * width, LANES)
        for k, ref in enumerate(state[:3]):
            out[k] = rows_of(ref, pl.ds(start, width))


def inner_kernel(at_ref, fields_ref, depth_ref, *refs):
    outs, (h_ref, head_ref, tail_ref), state = refs[:-7], refs[-7:-4], refs[-4:]
    n_rows = depth_ref.shape[0]
    for k in range(4):
        field = depth_ref[...] if k == 3 else fields_ref[0, k]
        state[k][...] = field
        head_ref[k] = field[:HALO]
        tail_ref[k] = field[n_rows - HALO :]
    model_steps(*state)
    h_ref[...] = state[0][HALO : n_rows - HALO]
    store_pieces(at_ref, outs, state, lambda ref, at: ref[HALO : n_rows - HALO, at])


def outer_kernel(at_ref, fields_ref, depth_ref, above_ref, below_ref, *refs):
    outs, h_ref, state = refs[:-5], refs[-5], refs[-4:]
    n_rows = depth_ref.shape[0]
    for k in range(4):
        state[k][:HALO] = above_ref[k]
        state[k][HALO : HALO + n_rows] = depth_ref[...] if k == 3 else fields_ref[0, k]
        state[k][HALO + n_rows :] = below_ref[k]
    model_steps(*state, at_ref[1].astype(jnp.float32), at_ref[2].astype(jnp.float32))

    def outer_rows(ref, at):
        return jnp.concatenate([ref[HALO : 2 * HALO, at], ref[n_rows : n_rows + HALO, at]], axis=0)

    h_ref[...] = outer_rows(state[0], pl.ds(0, depth_ref.shape[1]))
    store_pieces(at_ref, outs, state, outer_rows)


def forecast(kernel, name, at, arrays, n_rows, n_cols, count, window_rows, extra=()):
    shapes = [(3, n_rows, n_cols // count)] * count + [(n_rows, n_cols)] + list(extra)
    outs = pl.pallas_call(
        kernel,
        out_shape=[jax.ShapeDtypeStruct(shape, jnp.float32) for shape in shapes],
        in_specs=[in_smem] + [in_vmem] * len(arrays),
        out_specs=[in_vmem] * len(shapes),
        scratch_shapes=[pltpu.VMEM((window_rows, n_cols), jnp.float32)] * 4,
        compiler_params=pltpu.CompilerParams(vmem_limit_bytes=VMEM_BYTES),
        name=name,
    )(at, *arrays)
    return list(outs[:count]), outs[count:]


def misfit_kernel(at_ref, index_ref, value_ref, var_ref, inner_ref, outer_ref, out_ref, total_ref):
    inner_rows, n_cols = inner_ref.shape
    n_rows = inner_rows + 2 * HALO
    base = at_ref[3] * (n_rows * n_cols)
    row_in = lax.broadcasted_iota(jnp.int32, (8, LANES), 0)
    lane_in = lax.broadcasted_iota(jnp.int32, (8, LANES), 1)

    def tile(ref, row, col):
        first_row = pl.multiple_of(jnp.bitwise_and(row, -8), 8)
        first_col = pl.multiple_of(jnp.bitwise_and(col, -LANES), LANES)
        return ref[pl.ds(first_row, 8), pl.ds(first_col, LANES)]

    def point(k, carry):
        offset = index_ref[k] - base

        @pl.when(jnp.logical_and(offset >= 0, offset < n_rows * n_cols))
        def _():
            row = lax.div(offset, n_cols)
            col = offset - row * n_cols
            inner_row = row - HALO
            is_inner = jnp.logical_and(inner_row >= 0, inner_row < inner_rows)
            outer_row = jnp.where(row < HALO, row, row - inner_rows)
            hit = (row_in == jnp.bitwise_and(row, 7)) & (lane_in == jnp.bitwise_and(col, LANES - 1))

            def add(seen):
                total_ref[...] += jnp.where(hit, (value_ref[k] - seen) ** 2 / var_ref[k], 0.0)

            @pl.when(is_inner)
            def _():
                add(tile(inner_ref, inner_row, col))

            @pl.when(jnp.logical_not(is_inner))
            def _():
                add(tile(outer_ref, outer_row, col))

        return carry

    total_ref[...] = jnp.zeros_like(total_ref)
    lax.fori_loop(0, index_ref.shape[0], point, 0, unroll=8)
    out_ref[...] = jnp.broadcast_to(jnp.sum(total_ref[...]), out_ref.shape)


def misfit(at, obs_index, obs_value, obs_var, inner, outer):
    return pl.pallas_call(
        misfit_kernel,
        out_shape=jax.ShapeDtypeStruct((8, LANES), jnp.float32),
        in_specs=[in_smem] * 4 + [in_vmem] * 2,
        out_specs=in_vmem,
        scratch_shapes=[pltpu.VMEM((8, LANES), jnp.float32)],
        compiler_params=pltpu.CompilerParams(vmem_limit_bytes=VMEM_BYTES),
        name="misfit",
    )(at, obs_index, obs_value, obs_var, inner, outer)[0, 0]


def sum_over(x, axis):
    count = lax.axis_size(axis)
    step = 1
    while step < count:
        x = x + lax.ppermute(x, axis, [(i, i ^ step) for i in range(count)])
        step *= 2
    return x


def log_weight(loglik):
    slots = lax.broadcasted_iota(jnp.int32, (lax.axis_size("dom"),), 0)
    every = sum_over(jnp.where(slots == lax.axis_index("dom"), loglik, 0.0), "dom")
    peak = jnp.max(every)
    total = jnp.sum(jnp.exp(every - peak))
    return (loglik - (peak + jnp.log(total)))[None]


def place(at, pieces, spans, shape, into=None):
    count = len(pieces)
    n_cols = shape[-1]
    width = n_cols // count

    def kernel(at_ref, *refs):
        srcs = refs[:count]
        dst, sems = refs[-2], refs[-1]
        copies = []
        for m in range(count):
            first = pl.multiple_of(jnp.bitwise_xor(at_ref[0], m) * width, LANES)
            for s, (src_row, dst_row, size) in enumerate(spans):
                copies.append(
                    pltpu.make_async_copy(
                        srcs[m].at[:, pl.ds(src_row, size), :],
                        dst.at[0, :, pl.ds(dst_row, size), pl.ds(first, width)],
                        sems.at[m * len(spans) + s],
                    )
                )
        for c in copies:
            c.start()
        for c in copies:
            c.wait()

    extra = [] if into is None else [into]
    return pl.pallas_call(
        kernel,
        out_shape=pltpu.HBM(shape, jnp.float32),
        in_specs=[in_smem] + [in_vmem] * count + [in_hbm] * len(extra),
        out_specs=in_hbm,
        scratch_shapes=[pltpu.SemaphoreType.DMA((count * len(spans),))],
        input_output_aliases={} if into is None else {count + 1: 0},
        compiler_params=pltpu.CompilerParams(vmem_limit_bytes=VMEM_BYTES),
        name="place",
    )(at, *pieces, *extra)


def route_kernel(at_ref, parents_ref, out_ref, *, half):
    own = at_ref[0]
    side = at_ref[4]
    parents = [parents_ref[s] for s in range(2 * half)]

    def ranks(first):
        other = half - first
        running = jnp.int32(0)
        needed, rank = [], []
        for q in range(half):
            hit = jnp.int32(0)
            for s in range(half):
                hit = hit | jnp.where(parents[other + s] == first + q, 1, 0).astype(jnp.int32)
            needed.append(hit)
            rank.append(running)
            running = running + hit
        return needed, rank, running

    low = ranks(0)
    high = ranks(half)
    out_ref[0] = jnp.maximum(low[2], high[2])
    mine = [jnp.where(side == 0, a, b) for a, b in zip(low[0], high[0])]
    my_rank = [jnp.where(side == 0, a, b) for a, b in zip(low[1], high[1])]
    other_rank = [jnp.where(side == 0, b, a) for a, b in zip(low[1], high[1])]
    for k in range(half):
        chosen = jnp.int32(0)
        for q in range(half):
            chosen = jnp.where((mine[q] == 1) & (my_rank[q] == k), q, chosen)
        out_ref[1 + k] = jnp.bitwise_xor(chosen, own)
    for m in range(half):
        slot = jnp.bitwise_xor(own, m)
        parent = jnp.int32(0)
        for s in range(half):
            parent = jnp.where(slot == s, jnp.where(side == 0, parents[s], parents[half + s]), parent)
        local = parent - side * half
        remote = parent - (1 - side) * half
        from_rank = jnp.int32(0)
        for q in range(half):
            from_rank = jnp.where(remote == q, other_rank[q], from_rank)
        is_local = jnp.logical_and(local >= 0, local < half)
        out_ref[1 + half + m] = jnp.where(is_local, jnp.bitwise_xor(local, own), half + from_rank)


def route(at, parent_lookup, half):
    return pl.pallas_call(
        lambda *refs: route_kernel(*refs, half=half),
        out_shape=jax.ShapeDtypeStruct((1 + 2 * half,), jnp.int32),
        in_specs=[in_smem, in_smem],
        out_specs=in_smem,
        name="route",
    )(at, parent_lookup)


def to_mate(x, m):
    return lax.ppermute(x, "dom", [(i, i ^ m) for i in range(lax.axis_size("dom"))])


def among_mates(pieces):
    return [x if m == 0 else to_mate(x, m) for m, x in enumerate(pieces)]


def pick(routes, first, count, sources, stacks=(), stacked=False):
    block = sources[0].shape

    def kernel(routes_ref, *refs):
        n_in = len(sources) + len(stacks)
        srcs = [(ref, None) for ref in refs[: len(sources)]]
        srcs += [(ref, k) for ref in refs[len(sources) : n_in] for k in range(ref.shape[0])]
        for m in range(count):
            which = routes_ref[first + m]
            for s, (src, k) in enumerate(srcs):

                @pl.when(which == s)
                def _(m=m, src=src, k=k):
                    value = src[...] if k is None else src[k]
                    if stacked:
                        refs[n_in][m] = value
                    else:
                        refs[n_in + m][...] = value

    shapes = [(count,) + block] if stacked else [block] * count
    return pl.pallas_call(
        kernel,
        out_shape=[jax.ShapeDtypeStruct(shape, jnp.float32) for shape in shapes],
        in_specs=[in_smem] + [in_vmem] * (len(sources) + len(stacks)),
        out_specs=[in_vmem] * len(shapes),
        compiler_params=pltpu.CompilerParams(vmem_limit_bytes=VMEM_BYTES),
        name="pick",
    )(routes, *sources, *stacks)


def chosen(held, routes, crossing):
    return pick(routes, 1, crossing, held, stacked=True)[0]


def for_slots(held, got, routes):
    return pick(routes, 1 + len(held), len(held), held, [got])


def after(x, *earlier):
    return lax.optimization_barrier((x, earlier))[0]


def halo_rows(head, tail):
    count = lax.axis_size("rows")
    above = lax.ppermute(tail, "rows", [(i, i + 1) for i in range(count - 1)])
    below = lax.ppermute(head, "rows", [(i + 1, i) for i in range(count - 1)])
    return above, below


def inner_forecast(at, fields, depth, count):
    n_rows, n_cols = depth.shape
    rim = (4, HALO, n_cols)
    return forecast(inner_kernel, "inner", at, (fields, depth), n_rows - 2 * HALO, n_cols, count, n_rows, (rim, rim))


def outer_forecast(at, fields, depth, above, below, count):
    n_rows, n_cols = depth.shape
    arrays = (fields, depth, above, below)
    return forecast(outer_kernel, "outer", at, arrays, 2 * HALO, n_cols, count, n_rows + 2 * HALO)


def cycle(crossing, routes, at, fields, depth, obs_index, obs_value, obs_var):
    half = lax.axis_size("dom") // 2
    n_rows, n_cols = depth.shape
    inner, (inner_h, head, tail) = inner_forecast(at, fields, depth, half)
    above, below = halo_rows(head, tail)
    inner_held = among_mates(inner)
    outer, (outer_h,) = outer_forecast(at, fields, depth, above, below, half)
    outer_held = among_mates(outer)
    inner_chosen = chosen(after(inner_held, outer), routes, crossing)
    inner_got = to_mate(inner_chosen, half)
    misfit_sum = misfit(at, obs_index, obs_value, obs_var, inner_h, after(outer_h, inner_chosen))
    loglik = sum_over(-0.5 * misfit_sum, "rows")
    outer_chosen = chosen(after(outer_held, loglik), routes, crossing)
    outer_got = to_mate(outer_chosen, half)
    inner_done = among_mates(for_slots(inner_held, after(inner_got, outer_chosen), routes))
    log_weights = log_weight(after(loglik, outer_chosen))
    outer_slots = for_slots(outer_held, outer_got, routes)
    outer_done = among_mates(outer_slots)
    members = place(at, after(inner_done, outer_slots), ((0, HALO, n_rows - 2 * HALO),), fields.shape)
    members = place(at, outer_done, ((0, 0, HALO), (HALO, n_rows - HALO, HALO)), fields.shape, members)
    return log_weights, members


def shards(fields, depth, obs_index, obs_value, obs_var, parent_lookup):
    rows_at = lax.axis_index("rows")
    dom_at = lax.axis_index("dom")
    half = lax.axis_size("dom") // 2
    at = jnp.stack(
        [dom_at % half, rows_at > 0, rows_at < lax.axis_size("rows") - 1, rows_at, dom_at // half]
    ).astype(jnp.int32)
    if half == 4:
        routes = route(at, parent_lookup, half)
        branches = [
            (lambda r, a, *rest, c=c: cycle(c, r, a, *rest)) for c in range(1, half + 1)
        ]
        return lax.switch(
            jnp.clip(routes[0] - 1, 0, half - 1), branches, routes, at, fields, depth, obs_index, obs_value, obs_var
        )
    return by_pieces(at, fields, depth, obs_index, obs_value, obs_var, parent_lookup)


def by_pieces(at, fields, depth, obs_index, obs_value, obs_var, parent_lookup):
    pieces = lax.axis_size("dom")
    n_rows, n_cols = depth.shape
    whole = at * jnp.array([0, 1, 1, 1, 1], jnp.int32)
    (inner,), (inner_h, head, tail) = inner_forecast(whole, fields, depth, 1)
    (outer,), (outer_h,) = outer_forecast(whole, fields, depth, *halo_rows(head, tail), 1)
    misfit_sum = misfit(at, obs_index, obs_value, obs_var, inner_h, outer_h)
    log_weights = log_weight(sum_over(-0.5 * misfit_sum, "rows"))
    slab = jnp.concatenate([outer[:, :HALO], inner, outer[:, HALO:]], axis=1)
    tiles = slab.reshape(3, n_rows, pieces, n_cols // pieces).transpose(2, 0, 1, 3)
    received = lax.all_to_all(tiles, "dom", split_axis=0, concat_axis=0, tiled=True)
    picked = jnp.take(received, parent_lookup, axis=0, mode="clip")
    final = lax.all_to_all(picked, "dom", split_axis=0, concat_axis=0, tiled=True)
    return log_weights, final.transpose(1, 2, 0, 3).reshape(1, 3, n_rows, n_cols)


def solution(mesh):
    in_specs = (P("dom", None, "rows", None), P("rows", None), P(), P(), P(), P())
    out_specs = (P("dom"), P("dom", None, "rows", None))
    return jax.shard_map(shards, mesh=mesh, in_specs=in_specs, out_specs=out_specs, check_vma=False)
```

```python
import jax
import jax.numpy as jnp
from jax import lax
from jax.experimental import pallas as pl
from jax.experimental.pallas import tpu as pltpu
from jax.sharding import PartitionSpec as P

STEPS = 4
HALO = 2 * STEPS
LANES = 128
VMEM_BYTES = 48 * 2**20
ROUTED_HALF = 4

time_step = 0.5
coriolis = 0.2

in_vmem = pl.BlockSpec(memory_space=pltpu.VMEM)
in_smem = pl.BlockSpec(memory_space=pltpu.SMEM)
in_hbm = pl.BlockSpec(memory_space=pltpu.HBM)


def model_steps(h_ref, u_ref, v_ref, d_ref, top_open=None, bottom_open=None):
    n_rows, n_cols = h_ref.shape
    h_ref[...] = h_ref[...] * (0.5 * time_step)
    d_ref[...] = d_ref[...] * (0.25 * time_step * time_step)

    def cols(a):
        return pltpu.roll(a, n_cols - 1, 1) - pltpu.roll(a, 1, 1)

    def rows(a):
        return pltpu.roll(a, n_rows - 1, 0) - pltpu.roll(a, 1, 0)

    def step(_, carry):
        u = u_ref[...]
        v = v_ref[...]
        d = d_ref[...]
        h = h_ref[...] - (cols(d * u) + rows(d * v))
        if top_open is not None:
            h = jnp.concatenate(
                [h[:HALO] * top_open, h[HALO : n_rows - HALO], h[n_rows - HALO :] * bottom_open], axis=0
            )
        h_ref[...] = h
        u = u - cols(h) + (time_step * coriolis) * v
        u_ref[...] = u
        v_ref[...] = v - rows(h) - (time_step * coriolis) * u
        return carry

    lax.fori_loop(0, STEPS, step, 0)
    h_ref[...] = h_ref[...] * (2.0 / time_step)


def store_pieces(at_ref, outs, state, rows_of):
    width = outs[0].shape[-1]
    for m, out in enumerate(outs):
        start = pl.multiple_of(jnp.bitwise_xor(at_ref[0], m) * width, LANES)
        for k, ref in enumerate(state[:3]):
            out[k] = rows_of(ref, pl.ds(start, width))


def inner_kernel(at_ref, fields_ref, depth_ref, *refs):
    outs, h_ref, state = refs[:-5], refs[-5], refs[-4:]
    n_rows = depth_ref.shape[0]
    for k in range(4):
        state[k][...] = depth_ref[...] if k == 3 else fields_ref[0, k]
    model_steps(*state)
    h_ref[...] = state[0][HALO : n_rows - HALO]
    store_pieces(at_ref, outs, state, lambda ref, at: ref[HALO : n_rows - HALO, at])


def outer_kernel(at_ref, fields_ref, depth_ref, above_ref, below_ref, *refs):
    outs, h_ref, state = refs[:-5], refs[-5], refs[-4:]
    n_rows = depth_ref.shape[0]
    for k in range(4):
        state[k][:HALO] = above_ref[k]
        state[k][HALO : HALO + n_rows] = depth_ref[...] if k == 3 else fields_ref[0, k]
        state[k][HALO + n_rows :] = below_ref[k]
    model_steps(*state, at_ref[1].astype(jnp.float32), at_ref[2].astype(jnp.float32))

    def outer_rows(ref, at):
        return jnp.concatenate([ref[HALO : 2 * HALO, at], ref[n_rows : n_rows + HALO, at]], axis=0)

    h_ref[...] = outer_rows(state[0], pl.ds(0, depth_ref.shape[1]))
    store_pieces(at_ref, outs, state, outer_rows)


def forecast(kernel, name, at, arrays, n_rows, n_cols, count, window_rows):
    shapes = [(3, n_rows, n_cols // count)] * count + [(n_rows, n_cols)]
    outs = pl.pallas_call(
        kernel,
        out_shape=[jax.ShapeDtypeStruct(shape, jnp.float32) for shape in shapes],
        in_specs=[in_smem] + [in_vmem] * len(arrays),
        out_specs=[in_vmem] * len(shapes),
        scratch_shapes=[pltpu.VMEM((window_rows, n_cols), jnp.float32)] * 4,
        compiler_params=pltpu.CompilerParams(vmem_limit_bytes=VMEM_BYTES),
        name=name,
    )(at, *arrays)
    return list(outs[:count]), outs[count]


def misfit_kernel(at_ref, index_ref, value_ref, var_ref, inner_ref, outer_ref, out_ref, total_ref):
    inner_rows, n_cols = inner_ref.shape
    n_rows = inner_rows + 2 * HALO
    base = at_ref[3] * (n_rows * n_cols)
    row_in = lax.broadcasted_iota(jnp.int32, (8, LANES), 0)
    lane_in = lax.broadcasted_iota(jnp.int32, (8, LANES), 1)

    def tile(ref, row, col):
        first_row = pl.multiple_of(jnp.bitwise_and(row, -8), 8)
        first_col = pl.multiple_of(jnp.bitwise_and(col, -LANES), LANES)
        return ref[pl.ds(first_row, 8), pl.ds(first_col, LANES)]

    def point(k, carry):
        offset = index_ref[k] - base

        @pl.when(jnp.logical_and(offset >= 0, offset < n_rows * n_cols))
        def _():
            row = lax.div(offset, n_cols)
            col = offset - row * n_cols
            inner_row = row - HALO
            is_inner = jnp.logical_and(inner_row >= 0, inner_row < inner_rows)
            outer_row = jnp.where(row < HALO, row, row - inner_rows)
            hit = (row_in == jnp.bitwise_and(row, 7)) & (lane_in == jnp.bitwise_and(col, LANES - 1))

            def add(seen):
                total_ref[...] += jnp.where(hit, (value_ref[k] - seen) ** 2 / var_ref[k], 0.0)

            @pl.when(is_inner)
            def _():
                add(tile(inner_ref, inner_row, col))

            @pl.when(jnp.logical_not(is_inner))
            def _():
                add(tile(outer_ref, outer_row, col))

        return carry

    total_ref[...] = jnp.zeros_like(total_ref)
    lax.fori_loop(0, index_ref.shape[0], point, 0, unroll=8)
    lane = lax.broadcasted_iota(jnp.int32, out_ref.shape, 1)
    out_ref[...] = jnp.where(lane == at_ref[5], -0.5 * jnp.sum(total_ref[...]), 0.0)


def misfit(at, obs_index, obs_value, obs_var, inner, outer):
    return pl.pallas_call(
        misfit_kernel,
        out_shape=jax.ShapeDtypeStruct((1, LANES), jnp.float32),
        in_specs=[in_smem] * 4 + [in_vmem] * 2,
        out_specs=in_vmem,
        scratch_shapes=[pltpu.VMEM((8, LANES), jnp.float32)],
        compiler_params=pltpu.CompilerParams(vmem_limit_bytes=VMEM_BYTES),
        name="misfit",
    )(at, obs_index, obs_value, obs_var, inner, outer)


def sum_over(x, axis):
    count = lax.axis_size(axis)
    step = 1
    while step < count:
        x = x + lax.ppermute(x, axis, [(i, i ^ step) for i in range(count)])
        step *= 2
    return x


def weigh_kernel(at_ref, loglik_ref, out_ref, *, particles):
    lane = lax.broadcasted_iota(jnp.int32, loglik_ref.shape, 1)
    loglik = loglik_ref[...]
    peak = jnp.max(jnp.where(lane < particles, loglik, -jnp.inf), axis=1, keepdims=True)
    total = jnp.sum(jnp.where(lane < particles, jnp.exp(loglik - peak), 0.0), axis=1, keepdims=True)
    out_ref[0] = jnp.sum(jnp.where(lane == at_ref[5], loglik - (peak + jnp.log(total)), 0.0))


def log_weight(at, loglik):
    particles = lax.axis_size("dom")
    return pl.pallas_call(
        lambda *refs: weigh_kernel(*refs, particles=particles),
        out_shape=jax.ShapeDtypeStruct((1,), jnp.float32),
        in_specs=[in_smem, in_vmem],
        out_specs=in_smem,
        name="weigh",
    )(at, loglik)


def place(at, pieces, spans, shape, into=None):
    count = len(pieces)
    n_cols = shape[-1]
    width = n_cols // count

    def kernel(at_ref, *refs):
        srcs = refs[:count]
        dst, sems = refs[-2], refs[-1]
        copies = []
        for m in range(count):
            first = pl.multiple_of(jnp.bitwise_xor(at_ref[0], m) * width, LANES)
            for s, (src_row, dst_row, size) in enumerate(spans):
                copies.append(
                    pltpu.make_async_copy(
                        srcs[m].at[:, pl.ds(src_row, size), :],
                        dst.at[0, :, pl.ds(dst_row, size), pl.ds(first, width)],
                        sems.at[m * len(spans) + s],
                    )
                )
        for c in copies:
            c.start()
        for c in copies:
            c.wait()

    extra = [] if into is None else [into]
    return pl.pallas_call(
        kernel,
        out_shape=pltpu.HBM(shape, jnp.float32),
        in_specs=[in_smem] + [in_vmem] * count + [in_hbm] * len(extra),
        out_specs=in_hbm,
        scratch_shapes=[pltpu.SemaphoreType.DMA((count * len(spans),))],
        input_output_aliases={} if into is None else {count + 1: 0},
        compiler_params=pltpu.CompilerParams(vmem_limit_bytes=VMEM_BYTES),
        name="place",
    )(at, *pieces, *extra)


def prepare_kernel(at_ref, parents_ref, fields_ref, depth_ref, routes_ref, head_ref, tail_ref, sems, *, half):
    n_rows = depth_ref.shape[0]
    copies = []
    for ref, first in ((head_ref, 0), (tail_ref, n_rows - HALO)):
        rows = pl.ds(first, HALO)
        copies.append(pltpu.make_async_copy(fields_ref.at[0, :, rows], ref.at[pl.ds(0, 3)], sems.at[len(copies)]))
        copies.append(pltpu.make_async_copy(depth_ref.at[rows], ref.at[3], sems.at[len(copies)]))
    for c in copies:
        c.start()
    if half <= ROUTED_HALF:
        route(at_ref, parents_ref, routes_ref, half)
    for c in copies:
        c.wait()


def route(at_ref, parents_ref, out_ref, half):
    own = at_ref[0]
    side = at_ref[4]
    parents = [parents_ref[s] for s in range(2 * half)]

    def ranks(first):
        other = half - first
        running = jnp.int32(0)
        needed, rank = [], []
        for q in range(half):
            hit = jnp.int32(0)
            for s in range(half):
                hit = hit | jnp.where(parents[other + s] == first + q, 1, 0).astype(jnp.int32)
            needed.append(hit)
            rank.append(running)
            running = running + hit
        return needed, rank, running

    low = ranks(0)
    high = ranks(half)
    out_ref[0] = jnp.maximum(low[2], high[2])
    mine = [jnp.where(side == 0, a, b) for a, b in zip(low[0], high[0])]
    my_rank = [jnp.where(side == 0, a, b) for a, b in zip(low[1], high[1])]
    other_rank = [jnp.where(side == 0, b, a) for a, b in zip(low[1], high[1])]
    for k in range(half):
        chosen = jnp.int32(0)
        for q in range(half):
            chosen = jnp.where((mine[q] == 1) & (my_rank[q] == k), q, chosen)
        out_ref[1 + k] = jnp.bitwise_xor(chosen, own)
    for m in range(half):
        slot = jnp.bitwise_xor(own, m)
        parent = jnp.int32(0)
        for s in range(half):
            parent = jnp.where(slot == s, jnp.where(side == 0, parents[s], parents[half + s]), parent)
        local = parent - side * half
        remote = parent - (1 - side) * half
        from_rank = jnp.int32(0)
        for q in range(half):
            from_rank = jnp.where(remote == q, other_rank[q], from_rank)
        is_local = jnp.logical_and(local >= 0, local < half)
        out_ref[1 + half + m] = jnp.where(is_local, jnp.bitwise_xor(local, own), half + from_rank)


def prepare(at, parent_lookup, fields, depth, half):
    n_rows, n_cols = depth.shape
    rim = jax.ShapeDtypeStruct((4, HALO, n_cols), jnp.float32)
    return pl.pallas_call(
        lambda *refs: prepare_kernel(*refs, half=half),
        out_shape=[jax.ShapeDtypeStruct((1 + 2 * half,), jnp.int32), rim, rim],
        in_specs=[in_smem, in_smem, in_hbm, in_hbm],
        out_specs=[in_smem, in_vmem, in_vmem],
        scratch_shapes=[pltpu.SemaphoreType.DMA((4,))],
        compiler_params=pltpu.CompilerParams(vmem_limit_bytes=VMEM_BYTES),
        name="prepare",
    )(at, parent_lookup, fields, depth)


def to_mate(x, m):
    return lax.ppermute(x, "dom", [(i, i ^ m) for i in range(lax.axis_size("dom"))])


def among_mates(pieces):
    return [x if m == 0 else to_mate(x, m) for m, x in enumerate(pieces)]


def pick(routes, first, count, sources, stacks=(), stacked=False, cost=None):
    block = sources[0].shape

    def kernel(routes_ref, *refs):
        n_in = len(sources) + len(stacks)
        srcs = [(ref, None) for ref in refs[: len(sources)]]
        srcs += [(ref, k) for ref in refs[len(sources) : n_in] for k in range(ref.shape[0])]
        for m in range(count):
            which = routes_ref[first + m]
            for s, (src, k) in enumerate(srcs):

                @pl.when(which == s)
                def _(m=m, src=src, k=k):
                    value = src[...] if k is None else src[k]
                    if stacked:
                        refs[n_in][m] = value
                    else:
                        refs[n_in + m][...] = value

    shapes = [(count,) + block] if stacked else [block] * count
    return pl.pallas_call(
        kernel,
        out_shape=[jax.ShapeDtypeStruct(shape, jnp.float32) for shape in shapes],
        in_specs=[in_smem] + [in_vmem] * (len(sources) + len(stacks)),
        out_specs=[in_vmem] * len(shapes),
        compiler_params=pltpu.CompilerParams(vmem_limit_bytes=VMEM_BYTES),
        cost_estimate=cost,
        name="pick",
    )(routes, *sources, *stacks)


def chosen(held, routes, crossing, cost=None):
    return pick(routes, 1, crossing, held, stacked=True, cost=cost)[0]


def for_slots(held, got, routes):
    return pick(routes, 1 + len(held), len(held), held, [got])


def after(x, *earlier):
    return lax.optimization_barrier((x, earlier))[0]


def halo_rows(head, tail):
    count = lax.axis_size("rows")
    above = lax.ppermute(tail, "rows", [(i, i + 1) for i in range(count - 1)])
    below = lax.ppermute(head, "rows", [(i + 1, i) for i in range(count - 1)])
    return above, below


def inner_forecast(at, fields, depth, count):
    n_rows, n_cols = depth.shape
    return forecast(inner_kernel, "inner", at, (fields, depth), n_rows - 2 * HALO, n_cols, count, n_rows)


def outer_forecast(at, fields, depth, above, below, count):
    n_rows, n_cols = depth.shape
    arrays = (fields, depth, above, below)
    return forecast(outer_kernel, "outer", at, arrays, 2 * HALO, n_cols, count, n_rows + 2 * HALO)


def cycle(crossing, routes, head, tail, at, fields, depth, obs_index, obs_value, obs_var):
    half = lax.axis_size("dom") // 2
    n_rows, n_cols = depth.shape
    above, below = halo_rows(head, tail)
    inner, inner_h = inner_forecast(at, fields, depth, half)
    inner_held = among_mates(inner)
    outer, outer_h = outer_forecast(at, fields, depth, above, below, half)
    outer_held = among_mates(outer)
    inner_chosen = chosen(after(inner_held, outer), routes, crossing)
    inner_got = to_mate(inner_chosen, half)
    loglik = misfit(at, obs_index, obs_value, obs_var, inner_h, after(outer_h, inner_chosen))
    step = 1
    while step < half:
        loglik = loglik + to_mate(loglik, step)
        step *= 2
    outer_chosen = chosen(after(outer_held, loglik), routes, crossing)
    outer_got = to_mate(outer_chosen, half)
    loglik = loglik + to_mate(loglik, half)
    inner_done = among_mates(for_slots(inner_held, after(inner_got, outer_chosen), routes))
    outer_slots = for_slots(outer_held, outer_got, routes)
    outer_done = among_mates(outer_slots)
    log_weights = log_weight(at, sum_over(after(loglik, outer_slots), "rows"))
    members = place(at, after(inner_done, outer_slots), ((0, HALO, n_rows - 2 * HALO),), fields.shape)
    members = place(at, outer_done, ((0, 0, HALO), (HALO, n_rows - HALO, HALO)), fields.shape, members)
    return log_weights, members


def shards(fields, depth, obs_index, obs_value, obs_var, parent_lookup):
    rows_at = lax.axis_index("rows")
    dom_at = lax.axis_index("dom")
    half = lax.axis_size("dom") // 2
    at = jnp.stack(
        [dom_at % half, rows_at > 0, rows_at < lax.axis_size("rows") - 1, rows_at, dom_at // half, dom_at]
    ).astype(jnp.int32)
    routes, head, tail = prepare(at, parent_lookup, fields, depth, half)
    if half == ROUTED_HALF:
        branches = [(lambda *rest, c=c: cycle(c, *rest)) for c in range(1, half + 1)]
        crossing = jnp.clip(routes[0] - 1, 0, half - 1)
        return lax.switch(crossing, branches, routes, head, tail, at, fields, depth, obs_index, obs_value, obs_var)
    return by_pieces(head, tail, at, fields, depth, obs_index, obs_value, obs_var, parent_lookup)


def by_pieces(head, tail, at, fields, depth, obs_index, obs_value, obs_var, parent_lookup):
    pieces = lax.axis_size("dom")
    n_rows, n_cols = depth.shape
    whole = at * jnp.array([0, 1, 1, 1, 1, 1], jnp.int32)
    (inner,), inner_h = inner_forecast(whole, fields, depth, 1)
    (outer,), outer_h = outer_forecast(whole, fields, depth, *halo_rows(head, tail), 1)
    loglik = misfit(at, obs_index, obs_value, obs_var, inner_h, outer_h)
    log_weights = log_weight(at, sum_over(sum_over(loglik, "dom"), "rows"))
    slab = jnp.concatenate([outer[:, :HALO], inner, outer[:, HALO:]], axis=1)
    tiles = slab.reshape(3, n_rows, pieces, n_cols // pieces).transpose(2, 0, 1, 3)
    received = lax.all_to_all(tiles, "dom", split_axis=0, concat_axis=0, tiled=True)
    picked = jnp.take(received, parent_lookup, axis=0, mode="clip")
    final = lax.all_to_all(picked, "dom", split_axis=0, concat_axis=0, tiled=True)
    return log_weights, final.transpose(1, 2, 0, 3).reshape(1, 3, n_rows, n_cols)


def solution(mesh):
    in_specs = (P("dom", None, "rows", None), P("rows", None), P(), P(), P(), P())
    out_specs = (P("dom"), P("dom", None, "rows", None))
    return jax.shard_map(shards, mesh=mesh, in_specs=in_specs, out_specs=out_specs, check_vma=False)
```

```python
import jax
import jax.numpy as jnp
from jax import lax
from jax.experimental import pallas as pl
from jax.experimental.pallas import tpu as pltpu
from jax.sharding import PartitionSpec as P

STEPS = 4
HALO = 2 * STEPS
LANES = 128
VMEM_BYTES = 48 * 2**20
ROUTED_HALF = 4

time_step = 0.5
coriolis = 0.2

in_vmem = pl.BlockSpec(memory_space=pltpu.VMEM)
in_smem = pl.BlockSpec(memory_space=pltpu.SMEM)
in_hbm = pl.BlockSpec(memory_space=pltpu.HBM)


def model_steps(h_ref, u_ref, v_ref, d_ref, top_open=None, bottom_open=None):
    n_rows, n_cols = h_ref.shape
    h_ref[...] = h_ref[...] * (0.5 * time_step)
    d_ref[...] = d_ref[...] * (0.25 * time_step * time_step)

    def cols(a):
        return pltpu.roll(a, n_cols - 1, 1) - pltpu.roll(a, 1, 1)

    def rows(a):
        return pltpu.roll(a, n_rows - 1, 0) - pltpu.roll(a, 1, 0)

    def step(_, carry):
        u = u_ref[...]
        v = v_ref[...]
        d = d_ref[...]
        h = h_ref[...] - (cols(d * u) + rows(d * v))
        if top_open is not None:
            h = jnp.concatenate(
                [h[:HALO] * top_open, h[HALO : n_rows - HALO], h[n_rows - HALO :] * bottom_open], axis=0
            )
        h_ref[...] = h
        u = u - cols(h) + (time_step * coriolis) * v
        u_ref[...] = u
        v_ref[...] = v - rows(h) - (time_step * coriolis) * u
        return carry

    lax.fori_loop(0, STEPS, step, 0)
    h_ref[...] = h_ref[...] * (2.0 / time_step)


def store_pieces(at_ref, outs, state, rows_of):
    width = outs[0].shape[-1]
    for m, out in enumerate(outs):
        start = pl.multiple_of(jnp.bitwise_xor(at_ref[0], m) * width, LANES)
        for k, ref in enumerate(state[:3]):
            out[k] = rows_of(ref, pl.ds(start, width))


def inner_kernel(at_ref, fields_ref, depth_ref, *refs):
    outs, h_ref, state = refs[:-5], refs[-5], refs[-4:]
    n_rows = depth_ref.shape[0]
    for k in range(4):
        state[k][...] = depth_ref[...] if k == 3 else fields_ref[0, k]
    model_steps(*state)
    h_ref[...] = state[0][HALO : n_rows - HALO]
    store_pieces(at_ref, outs, state, lambda ref, at: ref[HALO : n_rows - HALO, at])


def outer_kernel(at_ref, fields_ref, depth_ref, above_ref, below_ref, *refs):
    outs, h_ref, state = refs[:-5], refs[-5], refs[-4:]
    n_rows = depth_ref.shape[0]
    for k in range(4):
        state[k][:HALO] = above_ref[k]
        state[k][HALO : HALO + n_rows] = depth_ref[...] if k == 3 else fields_ref[0, k]
        state[k][HALO + n_rows :] = below_ref[k]
    model_steps(*state, at_ref[1].astype(jnp.float32), at_ref[2].astype(jnp.float32))

    def outer_rows(ref, at):
        return jnp.concatenate([ref[HALO : 2 * HALO, at], ref[n_rows : n_rows + HALO, at]], axis=0)

    h_ref[...] = outer_rows(state[0], pl.ds(0, depth_ref.shape[1]))
    store_pieces(at_ref, outs, state, outer_rows)


def forecast(kernel, name, at, arrays, n_rows, n_cols, count, window_rows):
    shapes = [(3, n_rows, n_cols // count)] * count + [(n_rows, n_cols)]
    outs = pl.pallas_call(
        kernel,
        out_shape=[jax.ShapeDtypeStruct(shape, jnp.float32) for shape in shapes],
        in_specs=[in_smem] + [in_vmem] * len(arrays),
        out_specs=[in_vmem] * len(shapes),
        scratch_shapes=[pltpu.VMEM((window_rows, n_cols), jnp.float32)] * 4,
        compiler_params=pltpu.CompilerParams(vmem_limit_bytes=VMEM_BYTES),
        name=name,
    )(at, *arrays)
    return list(outs[:count]), outs[count]


def misfit_kernel(at_ref, index_ref, value_ref, var_ref, inner_ref, outer_ref, out_ref, total_ref):
    inner_rows, n_cols = inner_ref.shape
    n_rows = inner_rows + 2 * HALO
    base = at_ref[3] * (n_rows * n_cols)
    row_in = lax.broadcasted_iota(jnp.int32, (8, LANES), 0)
    lane_in = lax.broadcasted_iota(jnp.int32, (8, LANES), 1)

    def tile(ref, row, col):
        first_row = pl.multiple_of(jnp.bitwise_and(row, -8), 8)
        first_col = pl.multiple_of(jnp.bitwise_and(col, -LANES), LANES)
        return ref[pl.ds(first_row, 8), pl.ds(first_col, LANES)]

    def point(k, carry):
        offset = index_ref[k] - base

        @pl.when(jnp.logical_and(offset >= 0, offset < n_rows * n_cols))
        def _():
            row = lax.div(offset, n_cols)
            col = offset - row * n_cols
            inner_row = row - HALO
            is_inner = jnp.logical_and(inner_row >= 0, inner_row < inner_rows)
            outer_row = jnp.where(row < HALO, row, row - inner_rows)
            hit = (row_in == jnp.bitwise_and(row, 7)) & (lane_in == jnp.bitwise_and(col, LANES - 1))

            def add(seen):
                total_ref[...] += jnp.where(hit, (value_ref[k] - seen) ** 2 / var_ref[k], 0.0)

            @pl.when(is_inner)
            def _():
                add(tile(inner_ref, inner_row, col))

            @pl.when(jnp.logical_not(is_inner))
            def _():
                add(tile(outer_ref, outer_row, col))

        return carry

    total_ref[...] = jnp.zeros_like(total_ref)
    lax.fori_loop(0, index_ref.shape[0], point, 0, unroll=8)
    lane = lax.broadcasted_iota(jnp.int32, out_ref.shape, 1)
    out_ref[...] = jnp.where(lane == at_ref[5], -0.5 * jnp.sum(total_ref[...]), 0.0)


def misfit(at, obs_index, obs_value, obs_var, inner, outer):
    return pl.pallas_call(
        misfit_kernel,
        out_shape=jax.ShapeDtypeStruct((1, LANES), jnp.float32),
        in_specs=[in_smem] * 4 + [in_vmem] * 2,
        out_specs=in_vmem,
        scratch_shapes=[pltpu.VMEM((8, LANES), jnp.float32)],
        compiler_params=pltpu.CompilerParams(vmem_limit_bytes=VMEM_BYTES),
        name="misfit",
    )(at, obs_index, obs_value, obs_var, inner, outer)


def sum_over(x, axis):
    count = lax.axis_size(axis)
    step = 1
    while step < count:
        x = x + lax.ppermute(x, axis, [(i, i ^ step) for i in range(count)])
        step *= 2
    return x


def weigh_kernel(at_ref, loglik_ref, out_ref, *, particles):
    lane = lax.broadcasted_iota(jnp.int32, loglik_ref.shape, 1)
    loglik = loglik_ref[...]
    peak = jnp.max(jnp.where(lane < particles, loglik, -jnp.inf), axis=1, keepdims=True)
    total = jnp.sum(jnp.where(lane < particles, jnp.exp(loglik - peak), 0.0), axis=1, keepdims=True)
    out_ref[0] = jnp.sum(jnp.where(lane == at_ref[5], loglik - (peak + jnp.log(total)), 0.0))


def log_weight(at, loglik):
    particles = lax.axis_size("dom")
    return pl.pallas_call(
        lambda *refs: weigh_kernel(*refs, particles=particles),
        out_shape=jax.ShapeDtypeStruct((1,), jnp.float32),
        in_specs=[in_smem, in_vmem],
        out_specs=in_smem,
        name="weigh",
    )(at, loglik)


def place(at, pieces, spans, shape, into=None):
    count = len(pieces)
    n_cols = shape[-1]
    width = n_cols // count

    def kernel(at_ref, *refs):
        srcs = refs[:count]
        dst, sems = refs[-2], refs[-1]
        copies = []
        for m in range(count):
            first = pl.multiple_of(jnp.bitwise_xor(at_ref[0], m) * width, LANES)
            for s, (src_row, dst_row, size) in enumerate(spans):
                copies.append(
                    pltpu.make_async_copy(
                        srcs[m].at[:, pl.ds(src_row, size), :],
                        dst.at[0, :, pl.ds(dst_row, size), pl.ds(first, width)],
                        sems.at[m * len(spans) + s],
                    )
                )
        for c in copies:
            c.start()
        for c in copies:
            c.wait()

    extra = [] if into is None else [into]
    return pl.pallas_call(
        kernel,
        out_shape=pltpu.HBM(shape, jnp.float32),
        in_specs=[in_smem] + [in_vmem] * count + [in_hbm] * len(extra),
        out_specs=in_hbm,
        scratch_shapes=[pltpu.SemaphoreType.DMA((count * len(spans),))],
        input_output_aliases={} if into is None else {count + 1: 0},
        compiler_params=pltpu.CompilerParams(vmem_limit_bytes=VMEM_BYTES),
        name="place",
    )(at, *pieces, *extra)


def prepare_kernel(at_ref, parents_ref, fields_ref, depth_ref, routes_ref, head_ref, tail_ref, sems, *, half):
    n_rows = depth_ref.shape[0]
    copies = []
    for ref, first in ((head_ref, 0), (tail_ref, n_rows - HALO)):
        rows = pl.ds(first, HALO)
        copies.append(pltpu.make_async_copy(fields_ref.at[0, :, rows], ref.at[pl.ds(0, 3)], sems.at[len(copies)]))
        copies.append(pltpu.make_async_copy(depth_ref.at[rows], ref.at[3], sems.at[len(copies)]))
    for c in copies:
        c.start()
    if half <= ROUTED_HALF:
        route(at_ref, parents_ref, routes_ref, half)
    for c in copies:
        c.wait()


def route(at_ref, parents_ref, out_ref, half):
    own = at_ref[0]
    side = at_ref[4]
    parents = [parents_ref[s] for s in range(2 * half)]

    def ranks(first):
        other = half - first
        running = jnp.int32(0)
        needed, rank = [], []
        for q in range(half):
            hit = jnp.int32(0)
            for s in range(half):
                hit = hit | jnp.where(parents[other + s] == first + q, 1, 0).astype(jnp.int32)
            needed.append(hit)
            rank.append(running)
            running = running + hit
        return needed, rank, running

    low = ranks(0)
    high = ranks(half)
    out_ref[0] = jnp.maximum(low[2], high[2])
    mine = [jnp.where(side == 0, a, b) for a, b in zip(low[0], high[0])]
    my_rank = [jnp.where(side == 0, a, b) for a, b in zip(low[1], high[1])]
    other_rank = [jnp.where(side == 0, b, a) for a, b in zip(low[1], high[1])]
    for k in range(half):
        chosen = jnp.int32(0)
        for q in range(half):
            chosen = jnp.where((mine[q] == 1) & (my_rank[q] == k), q, chosen)
        out_ref[1 + k] = jnp.bitwise_xor(chosen, own)
    for m in range(half):
        slot = jnp.bitwise_xor(own, m)
        parent = jnp.int32(0)
        for s in range(half):
            parent = jnp.where(slot == s, jnp.where(side == 0, parents[s], parents[half + s]), parent)
        local = parent - side * half
        remote = parent - (1 - side) * half
        from_rank = jnp.int32(0)
        for q in range(half):
            from_rank = jnp.where(remote == q, other_rank[q], from_rank)
        is_local = jnp.logical_and(local >= 0, local < half)
        out_ref[1 + half + m] = jnp.where(is_local, jnp.bitwise_xor(local, own), half + from_rank)


def prepare(at, parent_lookup, fields, depth, half):
    n_rows, n_cols = depth.shape
    rim = jax.ShapeDtypeStruct((4, HALO, n_cols), jnp.float32)
    return pl.pallas_call(
        lambda *refs: prepare_kernel(*refs, half=half),
        out_shape=[jax.ShapeDtypeStruct((1 + 2 * half,), jnp.int32), rim, rim],
        in_specs=[in_smem, in_smem, in_hbm, in_hbm],
        out_specs=[in_smem, in_vmem, in_vmem],
        scratch_shapes=[pltpu.SemaphoreType.DMA((4,))],
        compiler_params=pltpu.CompilerParams(vmem_limit_bytes=VMEM_BYTES),
        name="prepare",
    )(at, parent_lookup, fields, depth)


def to_mate(x, m):
    return lax.ppermute(x, "dom", [(i, i ^ m) for i in range(lax.axis_size("dom"))])


def among_mates(pieces):
    return [x if m == 0 else to_mate(x, m) for m, x in enumerate(pieces)]


def pick(routes, first, count, sources, stacks=(), stacked=False, cost=None):
    block = sources[0].shape

    def kernel(routes_ref, *refs):
        n_in = len(sources) + len(stacks)
        srcs = [(ref, None) for ref in refs[: len(sources)]]
        srcs += [(ref, k) for ref in refs[len(sources) : n_in] for k in range(ref.shape[0])]
        for m in range(count):
            which = routes_ref[first + m]
            for s, (src, k) in enumerate(srcs):

                @pl.when(which == s)
                def _(m=m, src=src, k=k):
                    value = src[...] if k is None else src[k]
                    if stacked:
                        refs[n_in][m] = value
                    else:
                        refs[n_in + m][...] = value

    shapes = [(count,) + block] if stacked else [block] * count
    return pl.pallas_call(
        kernel,
        out_shape=[jax.ShapeDtypeStruct(shape, jnp.float32) for shape in shapes],
        in_specs=[in_smem] + [in_vmem] * (len(sources) + len(stacks)),
        out_specs=[in_vmem] * len(shapes),
        compiler_params=pltpu.CompilerParams(vmem_limit_bytes=VMEM_BYTES),
        cost_estimate=cost,
        name="pick",
    )(routes, *sources, *stacks)


def chosen(held, routes, crossing, cost=None):
    return pick(routes, 1, crossing, held, stacked=True, cost=cost)[0]


def for_slots(held, got, routes):
    return pick(routes, 1 + len(held), len(held), held, [got])


def after(x, *earlier):
    return lax.optimization_barrier((x, earlier))[0]


def halo_rows(head, tail):
    count = lax.axis_size("rows")
    above = lax.ppermute(tail, "rows", [(i, i + 1) for i in range(count - 1)])
    below = lax.ppermute(head, "rows", [(i + 1, i) for i in range(count - 1)])
    return above, below


def inner_forecast(at, fields, depth, count):
    n_rows, n_cols = depth.shape
    return forecast(inner_kernel, "inner", at, (fields, depth), n_rows - 2 * HALO, n_cols, count, n_rows)


def outer_forecast(at, fields, depth, above, below, count):
    n_rows, n_cols = depth.shape
    arrays = (fields, depth, above, below)
    return forecast(outer_kernel, "outer", at, arrays, 2 * HALO, n_cols, count, n_rows + 2 * HALO)


def cycle(crossing, routes, head, tail, at, fields, depth, obs_index, obs_value, obs_var):
    half = lax.axis_size("dom") // 2
    n_rows, n_cols = depth.shape
    above, below = halo_rows(head, tail)
    inner, inner_h = inner_forecast(at, fields, depth, half)
    inner_held = among_mates(inner)
    outer, outer_h = outer_forecast(at, fields, depth, above, below, half)
    outer_held = among_mates(outer)
    inner_chosen = chosen(after(inner_held, outer), routes, crossing)
    inner_got = to_mate(inner_chosen, half)
    loglik = misfit(at, obs_index, obs_value, obs_var, inner_h, after(outer_h, inner_chosen))
    step = 1
    while step < half:
        loglik = loglik + to_mate(loglik, step)
        step *= 2
    outer_chosen = chosen(after(outer_held, loglik), routes, crossing)
    outer_got = to_mate(outer_chosen, half)
    inner_done = among_mates(for_slots(inner_held, after(inner_got, outer_chosen), routes))
    outer_slots = for_slots(outer_held, outer_got, routes)
    outer_done = among_mates(outer_slots)
    loglik = after(sum_over(after(loglik, outer_chosen), "rows"), outer_slots)
    log_weights = log_weight(at, loglik + to_mate(loglik, half))
    members = place(at, after(inner_done, outer_slots), ((0, HALO, n_rows - 2 * HALO),), fields.shape)
    members = place(at, outer_done, ((0, 0, HALO), (HALO, n_rows - HALO, HALO)), fields.shape, members)
    return log_weights, members


def shards(fields, depth, obs_index, obs_value, obs_var, parent_lookup):
    rows_at = lax.axis_index("rows")
    dom_at = lax.axis_index("dom")
    half = lax.axis_size("dom") // 2
    at = jnp.stack(
        [dom_at % half, rows_at > 0, rows_at < lax.axis_size("rows") - 1, rows_at, dom_at // half, dom_at]
    ).astype(jnp.int32)
    routes, head, tail = prepare(at, parent_lookup, fields, depth, half)
    if half == ROUTED_HALF:
        branches = [(lambda *rest, c=c: cycle(c, *rest)) for c in range(1, half + 1)]
        crossing = jnp.clip(routes[0] - 1, 0, half - 1)
        return lax.switch(crossing, branches, routes, head, tail, at, fields, depth, obs_index, obs_value, obs_var)
    return by_pieces(head, tail, at, fields, depth, obs_index, obs_value, obs_var, parent_lookup)


def by_pieces(head, tail, at, fields, depth, obs_index, obs_value, obs_var, parent_lookup):
    pieces = lax.axis_size("dom")
    n_rows, n_cols = depth.shape
    whole = at * jnp.array([0, 1, 1, 1, 1, 1], jnp.int32)
    (inner,), inner_h = inner_forecast(whole, fields, depth, 1)
    (outer,), outer_h = outer_forecast(whole, fields, depth, *halo_rows(head, tail), 1)
    loglik = misfit(at, obs_index, obs_value, obs_var, inner_h, outer_h)
    log_weights = log_weight(at, sum_over(sum_over(loglik, "dom"), "rows"))
    slab = jnp.concatenate([outer[:, :HALO], inner, outer[:, HALO:]], axis=1)
    tiles = slab.reshape(3, n_rows, pieces, n_cols // pieces).transpose(2, 0, 1, 3)
    received = lax.all_to_all(tiles, "dom", split_axis=0, concat_axis=0, tiled=True)
    picked = jnp.take(received, parent_lookup, axis=0, mode="clip")
    final = lax.all_to_all(picked, "dom", split_axis=0, concat_axis=0, tiled=True)
    return log_weights, final.transpose(1, 2, 0, 3).reshape(1, 3, n_rows, n_cols)


def solution(mesh):
    in_specs = (P("dom", None, "rows", None), P("rows", None), P(), P(), P(), P())
    out_specs = (P("dom"), P("dom", None, "rows", None))
    return jax.shard_map(shards, mesh=mesh, in_specs=in_specs, out_specs=out_specs, check_vma=False)
```

```python
import jax
import jax.numpy as jnp
from jax import lax
from jax.experimental import pallas as pl
from jax.experimental.pallas import tpu as pltpu
from jax.sharding import PartitionSpec as P

STEPS = 4
HALO = 2 * STEPS
LANES = 128
VMEM_BYTES = 48 * 2**20
ROUTED_HALF = 4

time_step = 0.5
coriolis = 0.2

in_vmem = pl.BlockSpec(memory_space=pltpu.VMEM)
in_smem = pl.BlockSpec(memory_space=pltpu.SMEM)
in_hbm = pl.BlockSpec(memory_space=pltpu.HBM)


def model_steps(h_ref, u_ref, v_ref, d_ref, top_open=None, bottom_open=None):
    n_rows, n_cols = h_ref.shape
    h_ref[...] = h_ref[...] * (0.5 * time_step)
    d_ref[...] = d_ref[...] * (0.25 * time_step * time_step)

    def cols(a):
        return pltpu.roll(a, n_cols - 1, 1) - pltpu.roll(a, 1, 1)

    def rows(a):
        return pltpu.roll(a, n_rows - 1, 0) - pltpu.roll(a, 1, 0)

    def step(_, carry):
        u = u_ref[...]
        v = v_ref[...]
        d = d_ref[...]
        h = h_ref[...] - (cols(d * u) + rows(d * v))
        if top_open is not None:
            h = jnp.concatenate(
                [h[:HALO] * top_open, h[HALO : n_rows - HALO], h[n_rows - HALO :] * bottom_open], axis=0
            )
        h_ref[...] = h
        u = u - cols(h) + (time_step * coriolis) * v
        u_ref[...] = u
        v_ref[...] = v - rows(h) - (time_step * coriolis) * u
        return carry

    lax.fori_loop(0, STEPS, step, 0)
    h_ref[...] = h_ref[...] * (2.0 / time_step)


def store_pieces(at_ref, outs, state, rows_of):
    width = outs[0].shape[-1]
    for m, out in enumerate(outs):
        start = pl.multiple_of(jnp.bitwise_xor(at_ref[0], m) * width, LANES)
        for k, ref in enumerate(state[:3]):
            out[k] = rows_of(ref, pl.ds(start, width))


def inner_kernel(at_ref, fields_ref, depth_ref, *refs):
    outs, h_ref, state = refs[:-5], refs[-5], refs[-4:]
    n_rows = depth_ref.shape[0]
    for k in range(4):
        state[k][...] = depth_ref[...] if k == 3 else fields_ref[0, k]
    model_steps(*state)
    h_ref[...] = state[0][HALO : n_rows - HALO]
    store_pieces(at_ref, outs, state, lambda ref, at: ref[HALO : n_rows - HALO, at])


def outer_kernel(at_ref, fields_ref, depth_ref, above_ref, below_ref, *refs):
    outs, h_ref, state = refs[:-5], refs[-5], refs[-4:]
    n_rows = depth_ref.shape[0]
    for k in range(4):
        state[k][:HALO] = above_ref[k]
        state[k][HALO : HALO + n_rows] = depth_ref[...] if k == 3 else fields_ref[0, k]
        state[k][HALO + n_rows :] = below_ref[k]
    model_steps(*state, at_ref[1].astype(jnp.float32), at_ref[2].astype(jnp.float32))

    def outer_rows(ref, at):
        return jnp.concatenate([ref[HALO : 2 * HALO, at], ref[n_rows : n_rows + HALO, at]], axis=0)

    h_ref[...] = outer_rows(state[0], pl.ds(0, depth_ref.shape[1]))
    store_pieces(at_ref, outs, state, outer_rows)


def forecast(kernel, name, at, arrays, n_rows, n_cols, count, window_rows):
    shapes = [(3, n_rows, n_cols // count)] * count + [(n_rows, n_cols)]
    outs = pl.pallas_call(
        kernel,
        out_shape=[jax.ShapeDtypeStruct(shape, jnp.float32) for shape in shapes],
        in_specs=[in_smem] + [in_vmem] * len(arrays),
        out_specs=[in_vmem] * len(shapes),
        scratch_shapes=[pltpu.VMEM((window_rows, n_cols), jnp.float32)] * 4,
        compiler_params=pltpu.CompilerParams(vmem_limit_bytes=VMEM_BYTES),
        name=name,
    )(at, *arrays)
    return list(outs[:count]), outs[count]


def misfit_kernel(at_ref, index_ref, value_ref, var_ref, inner_ref, outer_ref, out_ref, total_ref):
    inner_rows, n_cols = inner_ref.shape
    n_rows = inner_rows + 2 * HALO
    base = at_ref[3] * (n_rows * n_cols)
    row_in = lax.broadcasted_iota(jnp.int32, (8, LANES), 0)
    lane_in = lax.broadcasted_iota(jnp.int32, (8, LANES), 1)

    def tile(ref, row, col):
        first_row = pl.multiple_of(jnp.bitwise_and(row, -8), 8)
        first_col = pl.multiple_of(jnp.bitwise_and(col, -LANES), LANES)
        return ref[pl.ds(first_row, 8), pl.ds(first_col, LANES)]

    def point(k, carry):
        offset = index_ref[k] - base

        @pl.when(jnp.logical_and(offset >= 0, offset < n_rows * n_cols))
        def _():
            row = lax.div(offset, n_cols)
            col = offset - row * n_cols
            inner_row = row - HALO
            is_inner = jnp.logical_and(inner_row >= 0, inner_row < inner_rows)
            outer_row = jnp.where(row < HALO, row, row - inner_rows)
            hit = (row_in == jnp.bitwise_and(row, 7)) & (lane_in == jnp.bitwise_and(col, LANES - 1))

            def add(seen):
                total_ref[...] += jnp.where(hit, (value_ref[k] - seen) ** 2 / var_ref[k], 0.0)

            @pl.when(is_inner)
            def _():
                add(tile(inner_ref, inner_row, col))

            @pl.when(jnp.logical_not(is_inner))
            def _():
                add(tile(outer_ref, outer_row, col))

        return carry

    total_ref[...] = jnp.zeros_like(total_ref)
    lax.fori_loop(0, index_ref.shape[0], point, 0, unroll=8)
    lane = lax.broadcasted_iota(jnp.int32, out_ref.shape, 1)
    out_ref[...] = jnp.where(lane == at_ref[5], -0.5 * jnp.sum(total_ref[...]), 0.0)


def misfit(at, obs_index, obs_value, obs_var, inner, outer):
    return pl.pallas_call(
        misfit_kernel,
        out_shape=jax.ShapeDtypeStruct((1, LANES), jnp.float32),
        in_specs=[in_smem] * 4 + [in_vmem] * 2,
        out_specs=in_vmem,
        scratch_shapes=[pltpu.VMEM((8, LANES), jnp.float32)],
        compiler_params=pltpu.CompilerParams(vmem_limit_bytes=VMEM_BYTES),
        name="misfit",
    )(at, obs_index, obs_value, obs_var, inner, outer)


def sum_over(x, axis):
    count = lax.axis_size(axis)
    step = 1
    while step < count:
        x = x + lax.ppermute(x, axis, [(i, i ^ step) for i in range(count)])
        step *= 2
    return x


def own_log_weight(loglik, own, particles):
    lane = lax.broadcasted_iota(jnp.int32, loglik.shape, 1)
    peak = jnp.max(jnp.where(lane < particles, loglik, -jnp.inf), axis=1, keepdims=True)
    total = jnp.sum(jnp.where(lane < particles, jnp.exp(loglik - peak), 0.0), axis=1, keepdims=True)
    return jnp.sum(jnp.where(lane == own, loglik - (peak + jnp.log(total)), 0.0))


def weigh_kernel(at_ref, loglik_ref, out_ref, *, particles):
    out_ref[0] = own_log_weight(loglik_ref[...], at_ref[5], particles)


def log_weight(at, loglik):
    particles = lax.axis_size("dom")
    return pl.pallas_call(
        lambda *refs: weigh_kernel(*refs, particles=particles),
        out_shape=jax.ShapeDtypeStruct((1,), jnp.float32),
        in_specs=[in_smem, in_vmem],
        out_specs=in_smem,
        name="weigh",
    )(at, loglik)


def place(at, pieces, spans, shape, into=None, shares=()):
    count = len(pieces)
    width = shape[-1] // count
    particles = lax.axis_size("dom")

    def kernel(at_ref, *refs):
        srcs = refs[:count]
        outs = refs[n_in : n_in + n_out]
        sems = refs[-1]
        copies = []
        for m in range(count):
            first = pl.multiple_of(jnp.bitwise_xor(at_ref[0], m) * width, LANES)
            for s, (src_row, dst_row, size) in enumerate(spans):
                copies.append(
                    pltpu.make_async_copy(
                        srcs[m].at[:, pl.ds(src_row, size), :],
                        outs[0].at[0, :, pl.ds(dst_row, size), pl.ds(first, width)],
                        sems.at[m * len(spans) + s],
                    )
                )
        for c in copies:
            c.start()
        if shares:
            loglik = sum(ref[...] for ref in refs[n_in - len(shares) : n_in])
            outs[1][0] = own_log_weight(loglik, at_ref[5], particles)
        for c in copies:
            c.wait()

    extra = [] if into is None else [into]
    n_in = count + len(extra) + len(shares)
    out_shape = [pltpu.HBM(shape, jnp.float32)] + [jax.ShapeDtypeStruct((1,), jnp.float32)] * bool(shares)
    n_out = len(out_shape)
    return pl.pallas_call(
        kernel,
        out_shape=out_shape,
        in_specs=[in_smem] + [in_vmem] * count + [in_hbm] * len(extra) + [in_vmem] * len(shares),
        out_specs=[in_hbm] + [in_smem] * bool(shares),
        scratch_shapes=[pltpu.SemaphoreType.DMA((count * len(spans),))],
        input_output_aliases={} if into is None else {count + 1: 0},
        compiler_params=pltpu.CompilerParams(vmem_limit_bytes=VMEM_BYTES),
        name="place",
    )(at, *pieces, *extra, *shares)


def prepare_kernel(at_ref, parents_ref, fields_ref, depth_ref, routes_ref, head_ref, tail_ref, sems, *, half):
    n_rows = depth_ref.shape[0]
    copies = []
    for ref, first in ((head_ref, 0), (tail_ref, n_rows - HALO)):
        rows = pl.ds(first, HALO)
        copies.append(pltpu.make_async_copy(fields_ref.at[0, :, rows], ref.at[pl.ds(0, 3)], sems.at[len(copies)]))
        copies.append(pltpu.make_async_copy(depth_ref.at[rows], ref.at[3], sems.at[len(copies)]))
    for c in copies:
        c.start()
    if half <= ROUTED_HALF:
        route(at_ref, parents_ref, routes_ref, half)
    for c in copies:
        c.wait()


def route(at_ref, parents_ref, out_ref, half):
    own = at_ref[0]
    side = at_ref[4]
    parents = [parents_ref[s] for s in range(2 * half)]

    def ranks(first):
        other = half - first
        running = jnp.int32(0)
        needed, rank = [], []
        for q in range(half):
            hit = jnp.int32(0)
            for s in range(half):
                hit = hit | jnp.where(parents[other + s] == first + q, 1, 0).astype(jnp.int32)
            needed.append(hit)
            rank.append(running)
            running = running + hit
        return needed, rank, running

    low = ranks(0)
    high = ranks(half)
    out_ref[0] = jnp.maximum(low[2], high[2])
    mine = [jnp.where(side == 0, a, b) for a, b in zip(low[0], high[0])]
    my_rank = [jnp.where(side == 0, a, b) for a, b in zip(low[1], high[1])]
    other_rank = [jnp.where(side == 0, b, a) for a, b in zip(low[1], high[1])]
    for k in range(half):
        chosen = jnp.int32(0)
        for q in range(half):
            chosen = jnp.where((mine[q] == 1) & (my_rank[q] == k), q, chosen)
        out_ref[1 + k] = jnp.bitwise_xor(chosen, own)
    for m in range(half):
        slot = jnp.bitwise_xor(own, m)
        parent = jnp.int32(0)
        for s in range(half):
            parent = jnp.where(slot == s, jnp.where(side == 0, parents[s], parents[half + s]), parent)
        local = parent - side * half
        remote = parent - (1 - side) * half
        from_rank = jnp.int32(0)
        for q in range(half):
            from_rank = jnp.where(remote == q, other_rank[q], from_rank)
        is_local = jnp.logical_and(local >= 0, local < half)
        out_ref[1 + half + m] = jnp.where(is_local, jnp.bitwise_xor(local, own), half + from_rank)


def prepare(at, parent_lookup, fields, depth, half):
    n_rows, n_cols = depth.shape
    rim = jax.ShapeDtypeStruct((4, HALO, n_cols), jnp.float32)
    return pl.pallas_call(
        lambda *refs: prepare_kernel(*refs, half=half),
        out_shape=[jax.ShapeDtypeStruct((1 + 2 * half,), jnp.int32), rim, rim],
        in_specs=[in_smem, in_smem, in_hbm, in_hbm],
        out_specs=[in_smem, in_vmem, in_vmem],
        scratch_shapes=[pltpu.SemaphoreType.DMA((4,))],
        compiler_params=pltpu.CompilerParams(vmem_limit_bytes=VMEM_BYTES),
        name="prepare",
    )(at, parent_lookup, fields, depth)


def to_mate(x, m):
    return lax.ppermute(x, "dom", [(i, i ^ m) for i in range(lax.axis_size("dom"))])


def among_mates(pieces):
    return [x if m == 0 else to_mate(x, m) for m, x in enumerate(pieces)]


def pick(routes, first, count, sources, stacks=(), stacked=False, cost=None):
    block = sources[0].shape

    def kernel(routes_ref, *refs):
        n_in = len(sources) + len(stacks)
        srcs = [(ref, None) for ref in refs[: len(sources)]]
        srcs += [(ref, k) for ref in refs[len(sources) : n_in] for k in range(ref.shape[0])]
        for m in range(count):
            which = routes_ref[first + m]
            for s, (src, k) in enumerate(srcs):

                @pl.when(which == s)
                def _(m=m, src=src, k=k):
                    value = src[...] if k is None else src[k]
                    if stacked:
                        refs[n_in][m] = value
                    else:
                        refs[n_in + m][...] = value

    shapes = [(count,) + block] if stacked else [block] * count
    return pl.pallas_call(
        kernel,
        out_shape=[jax.ShapeDtypeStruct(shape, jnp.float32) for shape in shapes],
        in_specs=[in_smem] + [in_vmem] * (len(sources) + len(stacks)),
        out_specs=[in_vmem] * len(shapes),
        compiler_params=pltpu.CompilerParams(vmem_limit_bytes=VMEM_BYTES),
        cost_estimate=cost,
        name="pick",
    )(routes, *sources, *stacks)


def chosen(held, routes, crossing, cost=None):
    return pick(routes, 1, crossing, held, stacked=True, cost=cost)[0]


def for_slots(held, got, routes):
    return pick(routes, 1 + len(held), len(held), held, [got])


def after(x, *earlier):
    return lax.optimization_barrier((x, earlier))[0]


def halo_rows(head, tail):
    count = lax.axis_size("rows")
    above = lax.ppermute(tail, "rows", [(i, i + 1) for i in range(count - 1)])
    below = lax.ppermute(head, "rows", [(i + 1, i) for i in range(count - 1)])
    return above, below


def inner_forecast(at, fields, depth, count):
    n_rows, n_cols = depth.shape
    return forecast(inner_kernel, "inner", at, (fields, depth), n_rows - 2 * HALO, n_cols, count, n_rows)


def outer_forecast(at, fields, depth, above, below, count):
    n_rows, n_cols = depth.shape
    arrays = (fields, depth, above, below)
    return forecast(outer_kernel, "outer", at, arrays, 2 * HALO, n_cols, count, n_rows + 2 * HALO)


def cycle(crossing, routes, head, tail, at, fields, depth, obs_index, obs_value, obs_var):
    half = lax.axis_size("dom") // 2
    n_rows, n_cols = depth.shape
    above, below = halo_rows(head, tail)
    inner, inner_h = inner_forecast(at, fields, depth, half)
    inner_held = among_mates(inner)
    outer, outer_h = outer_forecast(at, fields, depth, above, below, half)
    outer_held = among_mates(outer)
    inner_chosen = chosen(after(inner_held, outer), routes, crossing)
    inner_got = to_mate(inner_chosen, half)
    loglik = misfit(at, obs_index, obs_value, obs_var, inner_h, after(outer_h, inner_chosen))
    rows_first = crossing == 2
    if rows_first:
        loglik = sum_over(loglik, "rows")
    step = 1
    while step < half:
        loglik = loglik + to_mate(loglik, step)
        step *= 2
    outer_ready = after(outer_held, loglik) if rows_first else after(outer_held, loglik, inner_got)
    outer_chosen = chosen(outer_ready, routes, crossing)
    outer_got = to_mate(outer_chosen, half)
    inner_done = among_mates(for_slots(inner_held, after(inner_got, outer_chosen), routes))
    if not rows_first:
        loglik = sum_over(after(loglik, outer_chosen), "rows")
    outer_slots = for_slots(outer_held, outer_got, routes)
    outer_done = among_mates(outer_slots)
    loglik = after(loglik, outer_slots)
    shares = (loglik, to_mate(loglik, half))
    inner_rows = ((0, HALO, n_rows - 2 * HALO),)
    outer_rows = ((0, 0, HALO), (HALO, n_rows - HALO, HALO))
    (members,) = place(at, after(inner_done, outer_slots), inner_rows, fields.shape)
    members, log_weights = place(at, outer_done, outer_rows, fields.shape, members, shares)
    return log_weights, members


def shards(fields, depth, obs_index, obs_value, obs_var, parent_lookup):
    rows_at = lax.axis_index("rows")
    dom_at = lax.axis_index("dom")
    half = lax.axis_size("dom") // 2
    at = jnp.stack(
        [dom_at % half, rows_at > 0, rows_at < lax.axis_size("rows") - 1, rows_at, dom_at // half, dom_at]
    ).astype(jnp.int32)
    routes, head, tail = prepare(at, parent_lookup, fields, depth, half)
    if half == ROUTED_HALF:
        branches = [(lambda *rest, c=c: cycle(c, *rest)) for c in range(1, half + 1)]
        crossing = jnp.clip(routes[0] - 1, 0, half - 1)
        return lax.switch(crossing, branches, routes, head, tail, at, fields, depth, obs_index, obs_value, obs_var)
    return by_pieces(head, tail, at, fields, depth, obs_index, obs_value, obs_var, parent_lookup)


def by_pieces(head, tail, at, fields, depth, obs_index, obs_value, obs_var, parent_lookup):
    pieces = lax.axis_size("dom")
    n_rows, n_cols = depth.shape
    whole = at * jnp.array([0, 1, 1, 1, 1, 1], jnp.int32)
    (inner,), inner_h = inner_forecast(whole, fields, depth, 1)
    (outer,), outer_h = outer_forecast(whole, fields, depth, *halo_rows(head, tail), 1)
    loglik = misfit(at, obs_index, obs_value, obs_var, inner_h, outer_h)
    log_weights = log_weight(at, sum_over(sum_over(loglik, "dom"), "rows"))
    slab = jnp.concatenate([outer[:, :HALO], inner, outer[:, HALO:]], axis=1)
    tiles = slab.reshape(3, n_rows, pieces, n_cols // pieces).transpose(2, 0, 1, 3)
    received = lax.all_to_all(tiles, "dom", split_axis=0, concat_axis=0, tiled=True)
    picked = jnp.take(received, parent_lookup, axis=0, mode="clip")
    final = lax.all_to_all(picked, "dom", split_axis=0, concat_axis=0, tiled=True)
    return log_weights, final.transpose(1, 2, 0, 3).reshape(1, 3, n_rows, n_cols)


def solution(mesh):
    in_specs = (P("dom", None, "rows", None), P("rows", None), P(), P(), P(), P())
    out_specs = (P("dom"), P("dom", None, "rows", None))
    return jax.shard_map(shards, mesh=mesh, in_specs=in_specs, out_specs=out_specs, check_vma=False)
```

```python
import jax
import jax.numpy as jnp
from jax import lax
from jax.experimental import pallas as pl
from jax.experimental.pallas import tpu as pltpu
from jax.sharding import PartitionSpec as P

STEPS = 4
HALO = 2 * STEPS
LANES = 128
VMEM_BYTES = 48 * 2**20
ROUTED_HALF = 4

time_step = 0.5
coriolis = 0.2

in_vmem = pl.BlockSpec(memory_space=pltpu.VMEM)
in_smem = pl.BlockSpec(memory_space=pltpu.SMEM)
in_hbm = pl.BlockSpec(memory_space=pltpu.HBM)


def model_steps(h_ref, u_ref, v_ref, d_ref, top_open=None, bottom_open=None):
    n_rows, n_cols = h_ref.shape

    def cols(a):
        return pltpu.roll(a, n_cols - 1, 1) - pltpu.roll(a, 1, 1)

    def rows(a):
        return pltpu.roll(a, n_rows - 1, 0) - pltpu.roll(a, 1, 0)

    def step(_, carry):
        u = u_ref[...]
        v = v_ref[...]
        d = d_ref[...]
        h = h_ref[...] - (cols(d * u) + rows(d * v))
        if top_open is not None:
            h = jnp.concatenate(
                [h[:HALO] * top_open, h[HALO : n_rows - HALO], h[n_rows - HALO :] * bottom_open], axis=0
            )
        h_ref[...] = h
        u = u - cols(h) + (time_step * coriolis) * v
        u_ref[...] = u
        v_ref[...] = v - rows(h) - (time_step * coriolis) * u
        return carry

    lax.fori_loop(0, STEPS, step, 0)


def held(k, field):
    return field * {0: 0.5 * time_step, 3: 0.25 * time_step * time_step}[k] if k in (0, 3) else field


def freed(k, field):
    return field * (2.0 / time_step) if k == 0 else field


def store_pieces(at_ref, outs, state, rows_of):
    width = outs[0].shape[-1]
    for m, out in enumerate(outs):
        start = pl.multiple_of(jnp.bitwise_xor(at_ref[0], m) * width, LANES)
        for k, ref in enumerate(state[:3]):
            out[k] = freed(k, rows_of(ref, pl.ds(start, width)))


def inner_kernel(at_ref, fields_ref, depth_ref, *refs):
    outs, h_ref, state = refs[:-5], refs[-5], refs[-4:]
    n_rows = depth_ref.shape[0]
    for k in range(4):
        state[k][...] = held(k, depth_ref[...] if k == 3 else fields_ref[0, k])
    model_steps(*state)
    h_ref[...] = freed(0, state[0][HALO : n_rows - HALO])
    store_pieces(at_ref, outs, state, lambda ref, at: ref[HALO : n_rows - HALO, at])


def outer_kernel(at_ref, fields_ref, depth_ref, above_ref, below_ref, *refs):
    outs, h_ref, state = refs[:-5], refs[-5], refs[-4:]
    n_rows = depth_ref.shape[0]
    for k in range(4):
        state[k][:HALO] = held(k, above_ref[k])
        state[k][HALO : HALO + n_rows] = held(k, depth_ref[...] if k == 3 else fields_ref[0, k])
        state[k][HALO + n_rows :] = held(k, below_ref[k])
    model_steps(*state, at_ref[1].astype(jnp.float32), at_ref[2].astype(jnp.float32))

    def outer_rows(ref, at):
        return jnp.concatenate([ref[HALO : 2 * HALO, at], ref[n_rows : n_rows + HALO, at]], axis=0)

    h_ref[...] = freed(0, outer_rows(state[0], pl.ds(0, depth_ref.shape[1])))
    store_pieces(at_ref, outs, state, outer_rows)


def forecast(kernel, name, at, arrays, n_rows, n_cols, count, window_rows):
    shapes = [(3, n_rows, n_cols // count)] * count + [(n_rows, n_cols)]
    outs = pl.pallas_call(
        kernel,
        out_shape=[jax.ShapeDtypeStruct(shape, jnp.float32) for shape in shapes],
        in_specs=[in_smem] + [in_vmem] * len(arrays),
        out_specs=[in_vmem] * len(shapes),
        scratch_shapes=[pltpu.VMEM((window_rows, n_cols), jnp.float32)] * 4,
        compiler_params=pltpu.CompilerParams(vmem_limit_bytes=VMEM_BYTES),
        name=name,
    )(at, *arrays)
    return list(outs[:count]), outs[count]


def misfit_kernel(at_ref, index_ref, value_ref, var_ref, inner_ref, outer_ref, out_ref, total_ref):
    inner_rows, n_cols = inner_ref.shape
    n_rows = inner_rows + 2 * HALO
    base = at_ref[3] * (n_rows * n_cols)
    row_in = lax.broadcasted_iota(jnp.int32, (8, LANES), 0)
    lane_in = lax.broadcasted_iota(jnp.int32, (8, LANES), 1)

    def tile(ref, row, col):
        first_row = pl.multiple_of(jnp.bitwise_and(row, -8), 8)
        first_col = pl.multiple_of(jnp.bitwise_and(col, -LANES), LANES)
        return ref[pl.ds(first_row, 8), pl.ds(first_col, LANES)]

    def point(k, carry):
        offset = index_ref[k] - base

        @pl.when(jnp.logical_and(offset >= 0, offset < n_rows * n_cols))
        def _():
            row = lax.div(offset, n_cols)
            col = offset - row * n_cols
            inner_row = row - HALO
            is_inner = jnp.logical_and(inner_row >= 0, inner_row < inner_rows)
            outer_row = jnp.where(row < HALO, row, row - inner_rows)
            hit = (row_in == jnp.bitwise_and(row, 7)) & (lane_in == jnp.bitwise_and(col, LANES - 1))

            def add(seen):
                total_ref[...] += jnp.where(hit, (value_ref[k] - seen) ** 2 / var_ref[k], 0.0)

            @pl.when(is_inner)
            def _():
                add(tile(inner_ref, inner_row, col))

            @pl.when(jnp.logical_not(is_inner))
            def _():
                add(tile(outer_ref, outer_row, col))

        return carry

    total_ref[...] = jnp.zeros_like(total_ref)
    lax.fori_loop(0, index_ref.shape[0], point, 0, unroll=8)
    lane = lax.broadcasted_iota(jnp.int32, out_ref.shape, 1)
    out_ref[...] = jnp.where(lane == at_ref[5], -0.5 * jnp.sum(total_ref[...]), 0.0)


def misfit(at, obs_index, obs_value, obs_var, inner, outer):
    return pl.pallas_call(
        misfit_kernel,
        out_shape=jax.ShapeDtypeStruct((1, LANES), jnp.float32),
        in_specs=[in_smem] * 4 + [in_vmem] * 2,
        out_specs=in_vmem,
        scratch_shapes=[pltpu.VMEM((8, LANES), jnp.float32)],
        compiler_params=pltpu.CompilerParams(vmem_limit_bytes=VMEM_BYTES),
        name="misfit",
    )(at, obs_index, obs_value, obs_var, inner, outer)


def sum_over(x, axis):
    count = lax.axis_size(axis)
    step = 1
    while step < count:
        x = x + lax.ppermute(x, axis, [(i, i ^ step) for i in range(count)])
        step *= 2
    return x


def own_log_weight(loglik, own, particles):
    lane = lax.broadcasted_iota(jnp.int32, loglik.shape, 1)
    peak = jnp.max(jnp.where(lane < particles, loglik, -jnp.inf), axis=1, keepdims=True)
    total = jnp.sum(jnp.where(lane < particles, jnp.exp(loglik - peak), 0.0), axis=1, keepdims=True)
    return jnp.sum(jnp.where(lane == own, loglik - (peak + jnp.log(total)), 0.0))


def weigh_kernel(at_ref, loglik_ref, out_ref, *, particles):
    out_ref[0] = own_log_weight(loglik_ref[...], at_ref[5], particles)


def log_weight(at, loglik):
    particles = lax.axis_size("dom")
    return pl.pallas_call(
        lambda *refs: weigh_kernel(*refs, particles=particles),
        out_shape=jax.ShapeDtypeStruct((1,), jnp.float32),
        in_specs=[in_smem, in_vmem],
        out_specs=in_smem,
        name="weigh",
    )(at, loglik)


def place(at, pieces, spans, shape, into=None, shares=(), offset=0):
    count = len(pieces)
    width = pieces[0].shape[-1]
    stride = shape[-1] // count
    particles = lax.axis_size("dom")

    def kernel(at_ref, *refs):
        srcs = refs[:count]
        outs = refs[n_in : n_in + n_out]
        sems = refs[-1]
        copies = []
        for m in range(count):
            first = pl.multiple_of(jnp.bitwise_xor(at_ref[0], m) * stride + offset, LANES)
            for s, (src_row, dst_row, size) in enumerate(spans):
                copies.append(
                    pltpu.make_async_copy(
                        srcs[m].at[:, pl.ds(src_row, size), :],
                        outs[0].at[0, :, pl.ds(dst_row, size), pl.ds(first, width)],
                        sems.at[m * len(spans) + s],
                    )
                )
        for c in copies:
            c.start()
        if shares:
            loglik = sum(ref[...] for ref in refs[n_in - len(shares) : n_in])
            outs[1][0] = own_log_weight(loglik, at_ref[5], particles)
        for c in copies:
            c.wait()

    extra = [] if into is None else [into]
    n_in = count + len(extra) + len(shares)
    out_shape = [pltpu.HBM(shape, jnp.float32)] + [jax.ShapeDtypeStruct((1,), jnp.float32)] * bool(shares)
    n_out = len(out_shape)
    return pl.pallas_call(
        kernel,
        out_shape=out_shape,
        in_specs=[in_smem] + [in_vmem] * count + [in_hbm] * len(extra) + [in_vmem] * len(shares),
        out_specs=[in_hbm] + [in_smem] * bool(shares),
        scratch_shapes=[pltpu.SemaphoreType.DMA((count * len(spans),))],
        input_output_aliases={} if into is None else {count + 1: 0},
        compiler_params=pltpu.CompilerParams(vmem_limit_bytes=VMEM_BYTES),
        name="place",
    )(at, *pieces, *extra, *shares)


def prepare_kernel(at_ref, parents_ref, fields_ref, depth_ref, routes_ref, head_ref, tail_ref, table_ref, sems, *, half):
    n_rows = depth_ref.shape[0]
    table = pltpu.make_async_copy(parents_ref, table_ref, sems.at[4])
    table.start()
    copies = []
    for ref, first in ((head_ref, 0), (tail_ref, n_rows - HALO)):
        rows = pl.ds(first, HALO)
        copies.append(pltpu.make_async_copy(fields_ref.at[0, :, rows], ref.at[pl.ds(0, 3)], sems.at[len(copies)]))
        copies.append(pltpu.make_async_copy(depth_ref.at[rows], ref.at[3], sems.at[len(copies)]))
    for c in copies:
        c.start()
    table.wait()
    if half <= ROUTED_HALF:
        route(at_ref, table_ref, routes_ref, half)
    for c in copies:
        c.wait()


def route(at_ref, parents_ref, out_ref, half):
    own = at_ref[0]
    side = at_ref[4]
    parents = [parents_ref[s] for s in range(2 * half)]

    def ranks(first):
        other = half - first
        running = jnp.int32(0)
        needed, rank = [], []
        for q in range(half):
            hit = jnp.int32(0)
            for s in range(half):
                hit = hit | jnp.where(parents[other + s] == first + q, 1, 0).astype(jnp.int32)
            needed.append(hit)
            rank.append(running)
            running = running + hit
        return needed, rank, running

    low = ranks(0)
    high = ranks(half)
    out_ref[0] = jnp.maximum(low[2], high[2])
    mine = [jnp.where(side == 0, a, b) for a, b in zip(low[0], high[0])]
    my_rank = [jnp.where(side == 0, a, b) for a, b in zip(low[1], high[1])]
    other_rank = [jnp.where(side == 0, b, a) for a, b in zip(low[1], high[1])]
    for k in range(half):
        chosen = jnp.int32(0)
        for q in range(half):
            chosen = jnp.where((mine[q] == 1) & (my_rank[q] == k), q, chosen)
        out_ref[1 + k] = jnp.bitwise_xor(chosen, own)
    for m in range(half):
        slot = jnp.bitwise_xor(own, m)
        parent = jnp.int32(0)
        for s in range(half):
            parent = jnp.where(slot == s, jnp.where(side == 0, parents[s], parents[half + s]), parent)
        local = parent - side * half
        remote = parent - (1 - side) * half
        from_rank = jnp.int32(0)
        for q in range(half):
            from_rank = jnp.where(remote == q, other_rank[q], from_rank)
        is_local = jnp.logical_and(local >= 0, local < half)
        out_ref[1 + half + m] = jnp.where(is_local, jnp.bitwise_xor(local, own), half + from_rank)


def prepare(at, parent_lookup, fields, depth, half):
    n_rows, n_cols = depth.shape
    rim = jax.ShapeDtypeStruct((4, HALO, n_cols), jnp.float32)
    return pl.pallas_call(
        lambda *refs: prepare_kernel(*refs, half=half),
        out_shape=[jax.ShapeDtypeStruct((1 + 2 * half,), jnp.int32), rim, rim],
        in_specs=[in_smem, in_hbm, in_hbm, in_hbm],
        out_specs=[in_smem, in_vmem, in_vmem],
        scratch_shapes=[pltpu.SMEM(parent_lookup.shape, jnp.int32), pltpu.SemaphoreType.DMA((5,))],
        compiler_params=pltpu.CompilerParams(vmem_limit_bytes=VMEM_BYTES),
        name="prepare",
    )(at, parent_lookup, fields, depth)


def to_mate(x, m):
    return lax.ppermute(x, "dom", [(i, i ^ m) for i in range(lax.axis_size("dom"))])


def among_mates(pieces):
    return [x if m == 0 else to_mate(x, m) for m, x in enumerate(pieces)]


def pick(routes, first, count, sources, stacks=(), stacked=False, cost=None, columns=None):
    start, width = columns or (0, sources[0].shape[-1])
    block = sources[0].shape[:-1] + (width,)

    def kernel(routes_ref, *refs):
        n_in = len(sources) + len(stacks)
        srcs = [(ref, None) for ref in refs[: len(sources)]]
        srcs += [(ref, k) for ref in refs[len(sources) : n_in] for k in range(ref.shape[0])]
        for m in range(count):
            which = routes_ref[first + m]
            for s, (src, k) in enumerate(srcs):

                @pl.when(which == s)
                def _(m=m, src=src, k=k):
                    value = src[:, :, start : start + width] if k is None else src[k]
                    if stacked:
                        refs[n_in][m] = value
                    else:
                        refs[n_in + m][...] = value

    shapes = [(count,) + block] if stacked else [block] * count
    return pl.pallas_call(
        kernel,
        out_shape=[jax.ShapeDtypeStruct(shape, jnp.float32) for shape in shapes],
        in_specs=[in_smem] + [in_vmem] * (len(sources) + len(stacks)),
        out_specs=[in_vmem] * len(shapes),
        compiler_params=pltpu.CompilerParams(vmem_limit_bytes=VMEM_BYTES),
        cost_estimate=cost,
        name="pick",
    )(routes, *sources, *stacks)


def chosen(pieces, routes, crossing, columns=None):
    return pick(routes, 1, crossing, pieces, stacked=True, columns=columns)[0]


def for_slots(own, got, routes, columns=None):
    return pick(routes, 1 + len(own), len(own), own, [got], columns=columns)


def after(x, *earlier):
    return lax.optimization_barrier((x, earlier))[0]


def halo_rows(head, tail):
    count = lax.axis_size("rows")
    above = lax.ppermute(tail, "rows", [(i, i + 1) for i in range(count - 1)])
    below = lax.ppermute(head, "rows", [(i + 1, i) for i in range(count - 1)])
    return above, below


def inner_forecast(at, fields, depth, count):
    n_rows, n_cols = depth.shape
    return forecast(inner_kernel, "inner", at, (fields, depth), n_rows - 2 * HALO, n_cols, count, n_rows)


def outer_forecast(at, fields, depth, above, below, count):
    n_rows, n_cols = depth.shape
    arrays = (fields, depth, above, below)
    return forecast(outer_kernel, "outer", at, arrays, 2 * HALO, n_cols, count, n_rows + 2 * HALO)


def cycle(crossing, routes, head, tail, at, fields, depth, obs_index, obs_value, obs_var):
    half = lax.axis_size("dom") // 2
    n_rows, n_cols = depth.shape
    above, below = halo_rows(head, tail)
    inner, inner_h = inner_forecast(at, fields, depth, half)
    inner_held = among_mates(inner)
    outer, outer_h = outer_forecast(at, fields, depth, above, below, half)
    outer_held = among_mates(outer)
    inner_chosen = chosen(after(inner_held, outer), routes, crossing)
    inner_got = to_mate(inner_chosen, half)
    loglik = misfit(at, obs_index, obs_value, obs_var, inner_h, after(outer_h, inner_chosen))
    rows_first = crossing == 2
    if rows_first:
        loglik = sum_over(loglik, "rows")
    step = 1
    while step < half:
        loglik = loglik + to_mate(loglik, step)
        step *= 2
    outer_ready = after(outer_held, loglik) if rows_first else after(outer_held, loglik, inner_got)
    width = n_cols // half
    parts = [(0, width // 2), (width // 2, width // 2)] if crossing > 2 else [(0, width)]
    outer_chosen = [chosen(outer_ready, routes, crossing, columns) for columns in parts]
    outer_got = [to_mate(x, half) for x in outer_chosen]
    inner_done = among_mates(for_slots(inner_held, after(inner_got, *outer_chosen), routes))
    if not rows_first:
        loglik = sum_over(after(loglik, *outer_chosen), "rows")
    slots = []
    outer_done = []
    for got, columns in zip(outer_got, parts):
        slots.append(for_slots(outer_held, after(got, *slots), routes, columns))
        outer_done.append(among_mates(slots[-1]))
    loglik = after(loglik, slots[-1])
    shares = (loglik, to_mate(loglik, half))
    inner_rows = ((0, HALO, n_rows - 2 * HALO),)
    outer_rows = ((0, 0, HALO), (HALO, n_rows - HALO, HALO))
    (members,) = place(at, after(inner_done, slots[-1]), inner_rows, fields.shape)
    for done, (start, _) in zip(outer_done[:-1], parts):
        (members,) = place(at, done, outer_rows, fields.shape, members, (), start)
    members, log_weights = place(at, outer_done[-1], outer_rows, fields.shape, members, shares, parts[-1][0])
    return log_weights, members


def shards(fields, depth, obs_index, obs_value, obs_var, parent_lookup):
    rows_at = lax.axis_index("rows")
    dom_at = lax.axis_index("dom")
    half = lax.axis_size("dom") // 2
    at = jnp.stack(
        [dom_at % half, rows_at > 0, rows_at < lax.axis_size("rows") - 1, rows_at, dom_at // half, dom_at]
    ).astype(jnp.int32)
    routes, head, tail = prepare(at, parent_lookup, fields, depth, half)
    if half == ROUTED_HALF:
        branches = [(lambda *rest, c=c: cycle(c, *rest)) for c in range(1, half + 1)]
        crossing = jnp.clip(routes[0] - 1, 0, half - 1)
        return lax.switch(crossing, branches, routes, head, tail, at, fields, depth, obs_index, obs_value, obs_var)
    return by_pieces(head, tail, at, fields, depth, obs_index, obs_value, obs_var, parent_lookup)


def by_pieces(head, tail, at, fields, depth, obs_index, obs_value, obs_var, parent_lookup):
    pieces = lax.axis_size("dom")
    n_rows, n_cols = depth.shape
    whole = at * jnp.array([0, 1, 1, 1, 1, 1], jnp.int32)
    (inner,), inner_h = inner_forecast(whole, fields, depth, 1)
    (outer,), outer_h = outer_forecast(whole, fields, depth, *halo_rows(head, tail), 1)
    loglik = misfit(at, obs_index, obs_value, obs_var, inner_h, outer_h)
    log_weights = log_weight(at, sum_over(sum_over(loglik, "dom"), "rows"))
    slab = jnp.concatenate([outer[:, :HALO], inner, outer[:, HALO:]], axis=1)
    tiles = slab.reshape(3, n_rows, pieces, n_cols // pieces).transpose(2, 0, 1, 3)
    received = lax.all_to_all(tiles, "dom", split_axis=0, concat_axis=0, tiled=True)
    picked = jnp.take(received, parent_lookup, axis=0, mode="clip")
    final = lax.all_to_all(picked, "dom", split_axis=0, concat_axis=0, tiled=True)
    return log_weights, final.transpose(1, 2, 0, 3).reshape(1, 3, n_rows, n_cols)


def solution(mesh):
    in_specs = (P("dom", None, "rows", None), P("rows", None), P(), P(), P(), P())
    out_specs = (P("dom"), P("dom", None, "rows", None))
    return jax.shard_map(shards, mesh=mesh, in_specs=in_specs, out_specs=out_specs, check_vma=False)
```

```python
import jax
import jax.numpy as jnp
from jax import lax
from jax.experimental import pallas as pl
from jax.experimental.pallas import tpu as pltpu
from jax.sharding import PartitionSpec as P

STEPS = 4
HALO = 2 * STEPS
LANES = 128
VMEM_BYTES = 48 * 2**20
ROUTED_HALF = 4

time_step = 0.5
coriolis = 0.2

in_vmem = pl.BlockSpec(memory_space=pltpu.VMEM)
in_smem = pl.BlockSpec(memory_space=pltpu.SMEM)
in_hbm = pl.BlockSpec(memory_space=pltpu.HBM)


def model_steps(h_ref, u_ref, v_ref, d_ref, top_open=None, bottom_open=None):
    n_rows, n_cols = h_ref.shape

    def cols(a):
        return pltpu.roll(a, n_cols - 1, 1) - pltpu.roll(a, 1, 1)

    def rows(a):
        return pltpu.roll(a, n_rows - 1, 0) - pltpu.roll(a, 1, 0)

    def step(_, carry):
        u = u_ref[...]
        v = v_ref[...]
        d = d_ref[...]
        h = h_ref[...] - (cols(d * u) + rows(d * v))
        if top_open is not None:
            h = jnp.concatenate(
                [h[:HALO] * top_open, h[HALO : n_rows - HALO], h[n_rows - HALO :] * bottom_open], axis=0
            )
        h_ref[...] = h
        u = u - cols(h) + (time_step * coriolis) * v
        u_ref[...] = u
        v_ref[...] = v - rows(h) - (time_step * coriolis) * u
        return carry

    lax.fori_loop(0, STEPS, step, 0)


def held(k, field):
    return field * {0: 0.5 * time_step, 3: 0.25 * time_step * time_step}[k] if k in (0, 3) else field


def freed(k, field):
    return field * (2.0 / time_step) if k == 0 else field


def store_pieces(at_ref, outs, state, rows_of):
    width = outs[0].shape[-1]
    for m, out in enumerate(outs):
        start = pl.multiple_of(jnp.bitwise_xor(at_ref[0], m) * width, LANES)
        for k, ref in enumerate(state[:3]):
            out[k] = freed(k, rows_of(ref, pl.ds(start, width)))


def inner_kernel(at_ref, fields_ref, depth_ref, *refs):
    outs, h_ref, state = refs[:-5], refs[-5], refs[-4:]
    n_rows = depth_ref.shape[0]
    for k in range(4):
        state[k][...] = held(k, depth_ref[...] if k == 3 else fields_ref[0, k])
    model_steps(*state)
    h_ref[...] = freed(0, state[0][HALO : n_rows - HALO])
    store_pieces(at_ref, outs, state, lambda ref, at: ref[HALO : n_rows - HALO, at])


def outer_kernel(at_ref, fields_ref, depth_ref, above_ref, below_ref, *refs):
    outs, h_ref, state = refs[:-5], refs[-5], refs[-4:]
    n_rows = depth_ref.shape[0]
    for k in range(4):
        state[k][:HALO] = held(k, above_ref[k])
        state[k][HALO : HALO + n_rows] = held(k, depth_ref[...] if k == 3 else fields_ref[0, k])
        state[k][HALO + n_rows :] = held(k, below_ref[k])
    model_steps(*state, at_ref[1].astype(jnp.float32), at_ref[2].astype(jnp.float32))

    def outer_rows(ref, at):
        return jnp.concatenate([ref[HALO : 2 * HALO, at], ref[n_rows : n_rows + HALO, at]], axis=0)

    h_ref[...] = freed(0, outer_rows(state[0], pl.ds(0, depth_ref.shape[1])))
    store_pieces(at_ref, outs, state, outer_rows)


def forecast(kernel, name, at, arrays, n_rows, n_cols, count, window_rows):
    shapes = [(3, n_rows, n_cols // count)] * count + [(n_rows, n_cols)]
    outs = pl.pallas_call(
        kernel,
        out_shape=[jax.ShapeDtypeStruct(shape, jnp.float32) for shape in shapes],
        in_specs=[in_smem] + [in_vmem] * len(arrays),
        out_specs=[in_vmem] * len(shapes),
        scratch_shapes=[pltpu.VMEM((window_rows, n_cols), jnp.float32)] * 4,
        compiler_params=pltpu.CompilerParams(vmem_limit_bytes=VMEM_BYTES),
        name=name,
    )(at, *arrays)
    return list(outs[:count]), outs[count]


def misfit_kernel(at_ref, index_ref, value_ref, var_ref, inner_ref, outer_ref, out_ref, total_ref):
    inner_rows, n_cols = inner_ref.shape
    n_rows = inner_rows + 2 * HALO
    base = at_ref[3] * (n_rows * n_cols)
    row_in = lax.broadcasted_iota(jnp.int32, (8, LANES), 0)
    lane_in = lax.broadcasted_iota(jnp.int32, (8, LANES), 1)

    def tile(ref, row, col):
        first_row = pl.multiple_of(jnp.bitwise_and(row, -8), 8)
        first_col = pl.multiple_of(jnp.bitwise_and(col, -LANES), LANES)
        return ref[pl.ds(first_row, 8), pl.ds(first_col, LANES)]

    def point(k, carry):
        offset = index_ref[k] - base

        @pl.when(jnp.logical_and(offset >= 0, offset < n_rows * n_cols))
        def _():
            row = lax.div(offset, n_cols)
            col = offset - row * n_cols
            inner_row = row - HALO
            is_inner = jnp.logical_and(inner_row >= 0, inner_row < inner_rows)
            outer_row = jnp.where(row < HALO, row, row - inner_rows)
            hit = (row_in == jnp.bitwise_and(row, 7)) & (lane_in == jnp.bitwise_and(col, LANES - 1))

            def add(seen):
                total_ref[...] += jnp.where(hit, (value_ref[k] - seen) ** 2 / var_ref[k], 0.0)

            @pl.when(is_inner)
            def _():
                add(tile(inner_ref, inner_row, col))

            @pl.when(jnp.logical_not(is_inner))
            def _():
                add(tile(outer_ref, outer_row, col))

        return carry

    total_ref[...] = jnp.zeros_like(total_ref)
    lax.fori_loop(0, index_ref.shape[0], point, 0, unroll=8)
    lane = lax.broadcasted_iota(jnp.int32, out_ref.shape, 1)
    out_ref[...] = jnp.where(lane == at_ref[5], -0.5 * jnp.sum(total_ref[...]), 0.0)


def misfit(at, obs_index, obs_value, obs_var, inner, outer):
    return pl.pallas_call(
        misfit_kernel,
        out_shape=jax.ShapeDtypeStruct((1, LANES), jnp.float32),
        in_specs=[in_smem] * 4 + [in_vmem] * 2,
        out_specs=in_vmem,
        scratch_shapes=[pltpu.VMEM((8, LANES), jnp.float32)],
        compiler_params=pltpu.CompilerParams(vmem_limit_bytes=VMEM_BYTES),
        name="misfit",
    )(at, obs_index, obs_value, obs_var, inner, outer)


def sum_over(x, axis):
    count = lax.axis_size(axis)
    step = 1
    while step < count:
        x = x + lax.ppermute(x, axis, [(i, i ^ step) for i in range(count)])
        step *= 2
    return x


def own_log_weight(loglik, own, particles):
    lane = lax.broadcasted_iota(jnp.int32, loglik.shape, 1)
    peak = jnp.max(jnp.where(lane < particles, loglik, -jnp.inf), axis=1, keepdims=True)
    total = jnp.sum(jnp.where(lane < particles, jnp.exp(loglik - peak), 0.0), axis=1, keepdims=True)
    return jnp.sum(jnp.where(lane == own, loglik - (peak + jnp.log(total)), 0.0))


def weigh_kernel(at_ref, loglik_ref, out_ref, *, particles):
    out_ref[0] = own_log_weight(loglik_ref[...], at_ref[5], particles)


def log_weight(at, loglik):
    particles = lax.axis_size("dom")
    return pl.pallas_call(
        lambda *refs: weigh_kernel(*refs, particles=particles),
        out_shape=jax.ShapeDtypeStruct((1,), jnp.float32),
        in_specs=[in_smem, in_vmem],
        out_specs=in_smem,
        name="weigh",
    )(at, loglik)


def place(at, pieces, spans, shape, into=None, shares=(), offset=0):
    count = len(pieces)
    width = pieces[0].shape[-1]
    stride = shape[-1] // count
    particles = lax.axis_size("dom")

    def kernel(at_ref, *refs):
        srcs = refs[:count]
        outs = refs[n_in : n_in + n_out]
        sems = refs[-1]
        copies = []
        for m in range(count):
            first = pl.multiple_of(jnp.bitwise_xor(at_ref[0], m) * stride + offset, LANES)
            for s, (src_row, dst_row, size) in enumerate(spans):
                copies.append(
                    pltpu.make_async_copy(
                        srcs[m].at[:, pl.ds(src_row, size), :],
                        outs[0].at[0, :, pl.ds(dst_row, size), pl.ds(first, width)],
                        sems.at[m * len(spans) + s],
                    )
                )
        for c in copies:
            c.start()
        if shares:
            loglik = sum(ref[...] for ref in refs[n_in - len(shares) : n_in])
            outs[1][0] = own_log_weight(loglik, at_ref[5], particles)
        for c in copies:
            c.wait()

    extra = [] if into is None else [into]
    n_in = count + len(extra) + len(shares)
    out_shape = [pltpu.HBM(shape, jnp.float32)] + [jax.ShapeDtypeStruct((1,), jnp.float32)] * bool(shares)
    n_out = len(out_shape)
    return pl.pallas_call(
        kernel,
        out_shape=out_shape,
        in_specs=[in_smem] + [in_vmem] * count + [in_hbm] * len(extra) + [in_vmem] * len(shares),
        out_specs=[in_hbm] + [in_smem] * bool(shares),
        scratch_shapes=[pltpu.SemaphoreType.DMA((count * len(spans),))],
        input_output_aliases={} if into is None else {count + 1: 0},
        compiler_params=pltpu.CompilerParams(vmem_limit_bytes=VMEM_BYTES),
        name="place",
    )(at, *pieces, *extra, *shares)


def prepare_kernel(at_ref, parents_ref, fields_ref, depth_ref, routes_ref, head_ref, tail_ref, table_ref, sems, *, half):
    n_rows = depth_ref.shape[0]
    table = pltpu.make_async_copy(parents_ref, table_ref, sems.at[4])
    table.start()
    copies = []
    for ref, first in ((head_ref, 0), (tail_ref, n_rows - HALO)):
        rows = pl.ds(first, HALO)
        copies.append(pltpu.make_async_copy(fields_ref.at[0, :, rows], ref.at[pl.ds(0, 3)], sems.at[len(copies)]))
        copies.append(pltpu.make_async_copy(depth_ref.at[rows], ref.at[3], sems.at[len(copies)]))
    for c in copies:
        c.start()
    table.wait()
    if half <= ROUTED_HALF:
        route(at_ref, table_ref, routes_ref, half)
    for c in copies:
        c.wait()


def route(at_ref, parents_ref, out_ref, half):
    own = at_ref[0]
    side = at_ref[4]
    parents = [parents_ref[s] for s in range(2 * half)]

    def ranks(first):
        other = half - first
        running = jnp.int32(0)
        needed, rank = [], []
        for q in range(half):
            hit = jnp.int32(0)
            for s in range(half):
                hit = hit | jnp.where(parents[other + s] == first + q, 1, 0).astype(jnp.int32)
            needed.append(hit)
            rank.append(running)
            running = running + hit
        return needed, rank, running

    low = ranks(0)
    high = ranks(half)
    out_ref[0] = jnp.maximum(low[2], high[2])
    mine = [jnp.where(side == 0, a, b) for a, b in zip(low[0], high[0])]
    my_rank = [jnp.where(side == 0, a, b) for a, b in zip(low[1], high[1])]
    other_rank = [jnp.where(side == 0, b, a) for a, b in zip(low[1], high[1])]
    for k in range(half):
        chosen = jnp.int32(0)
        for q in range(half):
            chosen = jnp.where((mine[q] == 1) & (my_rank[q] == k), q, chosen)
        out_ref[1 + k] = jnp.bitwise_xor(chosen, own)
    for m in range(half):
        slot = jnp.bitwise_xor(own, m)
        parent = jnp.int32(0)
        for s in range(half):
            parent = jnp.where(slot == s, jnp.where(side == 0, parents[s], parents[half + s]), parent)
        local = parent - side * half
        remote = parent - (1 - side) * half
        from_rank = jnp.int32(0)
        for q in range(half):
            from_rank = jnp.where(remote == q, other_rank[q], from_rank)
        is_local = jnp.logical_and(local >= 0, local < half)
        out_ref[1 + half + m] = jnp.where(is_local, jnp.bitwise_xor(local, own), half + from_rank)


def prepare(at, parent_lookup, fields, depth, half):
    n_rows, n_cols = depth.shape
    rim = jax.ShapeDtypeStruct((4, HALO, n_cols), jnp.float32)
    return pl.pallas_call(
        lambda *refs: prepare_kernel(*refs, half=half),
        out_shape=[jax.ShapeDtypeStruct((1 + 2 * half,), jnp.int32), rim, rim],
        in_specs=[in_smem, in_hbm, in_hbm, in_hbm],
        out_specs=[in_smem, in_vmem, in_vmem],
        scratch_shapes=[pltpu.SMEM(parent_lookup.shape, jnp.int32), pltpu.SemaphoreType.DMA((5,))],
        compiler_params=pltpu.CompilerParams(vmem_limit_bytes=VMEM_BYTES),
        name="prepare",
    )(at, pltpu.with_memory_space_constraint(parent_lookup, pltpu.HBM), fields, depth)


def to_mate(x, m):
    return lax.ppermute(x, "dom", [(i, i ^ m) for i in range(lax.axis_size("dom"))])


def among_mates(pieces):
    return [x if m == 0 else to_mate(x, m) for m, x in enumerate(pieces)]


def pick(routes, first, count, sources, stacks=(), stacked=False, cost=None, columns=None):
    start, width = columns or (0, sources[0].shape[-1])
    block = sources[0].shape[:-1] + (width,)

    def kernel(routes_ref, *refs):
        n_in = len(sources) + len(stacks)
        srcs = [(ref, None) for ref in refs[: len(sources)]]
        srcs += [(ref, k) for ref in refs[len(sources) : n_in] for k in range(ref.shape[0])]
        for m in range(count):
            which = routes_ref[first + m]
            for s, (src, k) in enumerate(srcs):

                @pl.when(which == s)
                def _(m=m, src=src, k=k):
                    value = src[:, :, start : start + width] if k is None else src[k]
                    if stacked:
                        refs[n_in][m] = value
                    else:
                        refs[n_in + m][...] = value

    shapes = [(count,) + block] if stacked else [block] * count
    return pl.pallas_call(
        kernel,
        out_shape=[jax.ShapeDtypeStruct(shape, jnp.float32) for shape in shapes],
        in_specs=[in_smem] + [in_vmem] * (len(sources) + len(stacks)),
        out_specs=[in_vmem] * len(shapes),
        compiler_params=pltpu.CompilerParams(vmem_limit_bytes=VMEM_BYTES),
        cost_estimate=cost,
        name="pick",
    )(routes, *sources, *stacks)


def chosen(pieces, routes, crossing, columns=None):
    return pick(routes, 1, crossing, pieces, stacked=True, columns=columns)[0]


def for_slots(own, got, routes, columns=None):
    return pick(routes, 1 + len(own), len(own), own, [got], columns=columns)


def after(x, *earlier):
    return lax.optimization_barrier((x, earlier))[0]


def halo_rows(head, tail):
    count = lax.axis_size("rows")
    above = lax.ppermute(tail, "rows", [(i, i + 1) for i in range(count - 1)])
    below = lax.ppermute(head, "rows", [(i + 1, i) for i in range(count - 1)])
    return above, below


def inner_forecast(at, fields, depth, count):
    n_rows, n_cols = depth.shape
    return forecast(inner_kernel, "inner", at, (fields, depth), n_rows - 2 * HALO, n_cols, count, n_rows)


def outer_forecast(at, fields, depth, above, below, count):
    n_rows, n_cols = depth.shape
    arrays = (fields, depth, above, below)
    return forecast(outer_kernel, "outer", at, arrays, 2 * HALO, n_cols, count, n_rows + 2 * HALO)


def cycle(crossing, routes, head, tail, at, fields, depth, obs_index, obs_value, obs_var):
    half = lax.axis_size("dom") // 2
    n_rows, n_cols = depth.shape
    above, below = halo_rows(head, tail)
    inner, inner_h = inner_forecast(at, fields, depth, half)
    inner_held = among_mates(inner)
    outer, outer_h = outer_forecast(at, fields, depth, above, below, half)
    outer_held = among_mates(outer)
    inner_chosen = chosen(after(inner_held, outer), routes, crossing)
    inner_got = to_mate(inner_chosen, half)
    loglik = misfit(at, obs_index, obs_value, obs_var, inner_h, after(outer_h, inner_chosen))
    rows_first = crossing == 2
    if rows_first:
        loglik = sum_over(loglik, "rows")
    step = 1
    while step < half:
        loglik = loglik + to_mate(loglik, step)
        step *= 2
    outer_ready = after(outer_held, loglik) if rows_first else after(outer_held, loglik, inner_got)
    width = n_cols // half
    parts = [(0, width // 2), (width // 2, width // 2)] if crossing > 2 else [(0, width)]
    outer_chosen = [chosen(outer_ready, routes, crossing, columns) for columns in parts]
    outer_got = [to_mate(x, half) for x in outer_chosen]
    inner_done = among_mates(for_slots(inner_held, after(inner_got, *outer_chosen), routes))
    if not rows_first:
        loglik = sum_over(after(loglik, *outer_chosen), "rows")
    slots = []
    outer_done = []
    for got, columns in zip(outer_got, parts):
        slots.append(for_slots(outer_held, after(got, *slots), routes, columns))
        outer_done.append(among_mates(slots[-1]))
    loglik = after(loglik, slots[-1])
    shares = (loglik, to_mate(loglik, half))
    inner_rows = ((0, HALO, n_rows - 2 * HALO),)
    outer_rows = ((0, 0, HALO), (HALO, n_rows - HALO, HALO))
    (members,) = place(at, after(inner_done, slots[-1]), inner_rows, fields.shape)
    for done, (start, _) in zip(outer_done[:-1], parts):
        (members,) = place(at, done, outer_rows, fields.shape, members, (), start)
    members, log_weights = place(at, outer_done[-1], outer_rows, fields.shape, members, shares, parts[-1][0])
    return log_weights, members


def shards(fields, depth, obs_index, obs_value, obs_var, parent_lookup):
    rows_at = lax.axis_index("rows")
    dom_at = lax.axis_index("dom")
    half = lax.axis_size("dom") // 2
    at = jnp.stack(
        [dom_at % half, rows_at > 0, rows_at < lax.axis_size("rows") - 1, rows_at, dom_at // half, dom_at]
    ).astype(jnp.int32)
    routes, head, tail = prepare(at, parent_lookup, fields, depth, half)
    if half == ROUTED_HALF:
        branches = [(lambda *rest, c=c: cycle(c, *rest)) for c in range(1, half + 1)]
        crossing = jnp.clip(routes[0] - 1, 0, half - 1)
        return lax.switch(crossing, branches, routes, head, tail, at, fields, depth, obs_index, obs_value, obs_var)
    return by_pieces(head, tail, at, fields, depth, obs_index, obs_value, obs_var, parent_lookup)


def by_pieces(head, tail, at, fields, depth, obs_index, obs_value, obs_var, parent_lookup):
    pieces = lax.axis_size("dom")
    n_rows, n_cols = depth.shape
    whole = at * jnp.array([0, 1, 1, 1, 1, 1], jnp.int32)
    (inner,), inner_h = inner_forecast(whole, fields, depth, 1)
    (outer,), outer_h = outer_forecast(whole, fields, depth, *halo_rows(head, tail), 1)
    loglik = misfit(at, obs_index, obs_value, obs_var, inner_h, outer_h)
    log_weights = log_weight(at, sum_over(sum_over(loglik, "dom"), "rows"))
    slab = jnp.concatenate([outer[:, :HALO], inner, outer[:, HALO:]], axis=1)
    tiles = slab.reshape(3, n_rows, pieces, n_cols // pieces).transpose(2, 0, 1, 3)
    received = lax.all_to_all(tiles, "dom", split_axis=0, concat_axis=0, tiled=True)
    picked = jnp.take(received, parent_lookup, axis=0, mode="clip")
    final = lax.all_to_all(picked, "dom", split_axis=0, concat_axis=0, tiled=True)
    return log_weights, final.transpose(1, 2, 0, 3).reshape(1, 3, n_rows, n_cols)


def solution(mesh):
    in_specs = (P("dom", None, "rows", None), P("rows", None), P(), P(), P(), P())
    out_specs = (P("dom"), P("dom", None, "rows", None))
    return jax.shard_map(shards, mesh=mesh, in_specs=in_specs, out_specs=out_specs, check_vma=False)
```
